32 devices in a mesh: feat: 4 (over y, x), dom: 8 (over z, core).
Axes of the slice: x: 2, y: 2, z: 4, core: 2. Of those that a mesh axis runs over, the one named last changes fastest.
Arguments:
- features: bfloat16 [4, 8, 512, 1024], P(None, 'dom', None, 'feat'), may hold values from -100 to 100
- w_self: bfloat16 [1024, 256], P('feat'), may hold values from -0.1875 to 0.1875
- w_neigh: bfloat16 [1024, 256], P('feat'), may hold values from -2 to 2
- gain: float32 [256], replicated, may hold values from 0.5 to 1.5
- shift: float32 [256], replicated, may hold values from -1 to 1
- d_hidden: bfloat16 [4, 8, 512, 256], P('feat', 'dom'), may hold values from -32 to 32
- send_rows: int32 [4, 8, 32, 32], P('feat', 'dom'), may hold values from 0 to 511
- send_count: int32 [4, 8, 32], P('feat', 'dom'), may hold values from 0 to 32, as said below
- tile_src: int32 [4, 8, 136], P('feat', 'dom'), may hold values from 0 to 11, as said below
- tile_dst: int32 [4, 8, 136], P('feat', 'dom'), may hold values from 0 to 3
- tile_count: int32 [4, 8], P('feat', 'dom'), may hold values from 12 to 136, as said below
- tile_vals: bfloat16 [4, 8, 136, 128, 128], P('feat', 'dom'), may hold values from 0 to 1, as said below
Outputs:
- hidden: bfloat16 [4, 8, 512, 256], P('feat', 'dom')
- d_self: bfloat16 [4, 8, 512, 256], P('feat', 'dom')
- d_neigh: bfloat16 [4, 8, 512, 256], P('feat', 'dom')
- gain_grad: float32 [256], replicated
- shift_grad: float32 [256], replicated
The draws below stay inside these ranges and needn't reach their ends.
Inputs may be any that keep to these rules, and one draw needn't show every extreme that they name: `send_rows`: rows may repeat within a list. `send_count`: the live slots are the first ones; in every draw some receiving partition gets 32 live slots from every partition. `tile_src`: blocks below 4 are the partition's own nodes, the others the halo rows in order of sender and slot; the first 12 tiles of each partition name every source block once. `tile_count`: the live tiles are the first ones; some partition has all 136 live. `tile_vals`: nonnegative; tiles past a partition's count are not used.
All inputs are finite; a program needn't handle non-finite values.
Results may differ from the reference program's by a relative error of at most 0.0056.
Values may be sent and summed in bfloat16 or wider, within the bound.
A program may use at most 64 MiB of HBM per device.

```python
import jax
import jax.numpy as jnp
from jax import lax

F = 1024
HID = 256
TILE = 128
ROWS_DEV = 512
SLOTS = 32
FGROUPS = 4
DGROUPS = 8
PARTS_SIZE = 32
NODES = 16384
LOCAL_BLOCKS = 4
HALO_ROWS = 1024
SRC_BLOCKS = 12
TILES = 136


def partition_ramp():
    position = jnp.arange(FGROUPS)[:, None] * DGROUPS + jnp.arange(DGROUPS)[None, :]
    return (3.0 ** (position.astype(jnp.float32) / (PARTS_SIZE - 1)))[:, :, None, None]


def draw_features(key, part):
    subkeys = jax.random.split(jax.random.fold_in(key, 101), 3)
    full_shape = (FGROUPS, DGROUPS, ROWS_DEV, F)
    row_scale = jnp.exp(jax.random.uniform(subkeys[1], (FGROUPS, DGROUPS, ROWS_DEV, 1), minval=0.0, maxval=jnp.log(10.0)))
    col_scale = jnp.exp(jax.random.uniform(subkeys[2], (F,), minval=0.0, maxval=jnp.log(10.0)))
    noise = jax.random.truncated_normal(subkeys[0], -4.0, 4.0, full_shape)
    result = noise * row_scale * col_scale * partition_ramp() / 30.0
    return jnp.clip(result, -100.0, 100.0).astype(jnp.bfloat16)


def draw_d_hidden(key, part):
    subkeys = jax.random.split(jax.random.fold_in(key, 202), 3)
    full_shape = (FGROUPS, DGROUPS, ROWS_DEV, HID)
    column_bias = jax.random.uniform(subkeys[1], (HID,), minval=-1.0, maxval=1.0)
    row_scale = jnp.exp(jax.random.uniform(subkeys[2], (FGROUPS, DGROUPS, ROWS_DEV, 1), minval=0.0, maxval=jnp.log(4.0)))
    noise = jax.random.truncated_normal(subkeys[0], -4.0, 4.0, full_shape)
    result = (column_bias + noise) * row_scale * partition_ramp() / 2.0
    return jnp.clip(result, -32.0, 32.0).astype(jnp.bfloat16)


def draw_send_count(key, part):
    subkeys = jax.random.split(jax.random.fold_in(key, 303), 2)
    counts = jax.random.randint(subkeys[0], (FGROUPS, DGROUPS, PARTS_SIZE), 0, SLOTS + 1)
    busiest = jax.random.randint(subkeys[1], (), 0, PARTS_SIZE)
    counts = jnp.where(jnp.arange(PARTS_SIZE)[None, None, :] == busiest, SLOTS, counts)
    return counts.astype(jnp.int32)


def one_order(subkey):
    return jax.random.permutation(subkey, SRC_BLOCKS)


def draw_tile_src(key, part):
    subkeys = jax.random.split(jax.random.fold_in(key, 404), 2)
    orders = jax.vmap(one_order)(jax.random.split(subkeys[0], PARTS_SIZE))
    others = jax.random.randint(subkeys[1], (PARTS_SIZE, TILES - SRC_BLOCKS), 0, SRC_BLOCKS)
    return jnp.concatenate([orders.astype(jnp.int32), others.astype(jnp.int32)], axis=1).reshape(FGROUPS, DGROUPS, TILES)


def draw_tile_count(key, part):
    subkeys = jax.random.split(jax.random.fold_in(key, 505), 2)
    room = TILES - SRC_BLOCKS
    picks = jax.random.randint(subkeys[0], (PARTS_SIZE,), 0, room + 1)
    extra = picks * picks // max(room, 1)
    busiest = jax.random.randint(subkeys[1], (), 0, PARTS_SIZE)
    extra = jnp.where(jnp.arange(PARTS_SIZE) == busiest, room, extra)
    return (SRC_BLOCKS + extra).reshape(FGROUPS, DGROUPS).astype(jnp.int32)


def draw_tile_vals(key, part):
    subkeys = jax.random.split(jax.random.fold_in(key, 606), 2)
    full_shape = (FGROUPS, DGROUPS, TILES, TILE, TILE)
    present = jax.random.uniform(subkeys[0], full_shape) < 0.0625
    weights = jax.random.uniform(subkeys[1], full_shape, minval=0.25, maxval=1.0)
    return jnp.where(present, weights, 0.0).astype(jnp.bfloat16)


def set_ends(values, key, smallest, top_value):
    extent = values.shape
    spot = [jax.random.randint(jax.random.fold_in(key, axis), (), 0, extent[axis]) for axis in range(len(extent))]
    values = values.at[tuple(spot)].set(smallest)
    longest = extent.index(max(extent))
    spot[longest] = (spot[longest] + 1) % extent[longest]
    return values.at[tuple(spot)].set(top_value)


def shard_levels(rng, dims, shards, smallest, high):
    loudness, own = 1.0, jax.random.fold_in(rng, 6)
    for axis_at, parts in shards:
        steps = jnp.exp(jax.random.uniform(jax.random.fold_in(own, axis_at), (parts,), jnp.float32, smallest / len(shards), high / len(shards)))
        loudness = loudness * jnp.repeat(steps, dims[axis_at] // parts).reshape([-1 if axis == axis_at else 1 for axis in range(len(dims))])
    return loudness


def bell_draw(stream_key, dims, width, limit, pieces=(), held_as=jnp.bfloat16):
    values = jax.random.normal(stream_key, dims, jnp.float32) * width
    if len(pieces) > 0:
        values = shard_levels(stream_key, dims, pieces, -0.22, 0.18) * values
    return jnp.clip(values, min=-limit, max=limit).astype(held_as)


def setup_inputs(seed: int = 0) -> dict:
    key_list = jax.random.split(jax.random.key(seed), 13)
    return {
        "features": draw_features(jax.random.fold_in(key_list[12], 71), 0),
        "w_self": bell_draw(key_list[1], (F, HID), F ** -0.5, 0.1875, ((0, 4),)),
        "w_neigh": bell_draw(key_list[2], (F, HID), (max(F // 128, 1)) ** -0.5, 2.0, ((0, 4),)),
        "gain": jnp.clip(1.0 + 0.1 * jax.random.normal(key_list[3], (HID,), jnp.float32), 0.5, 1.5),
        "shift": jnp.clip(jax.random.uniform(key_list[4], (HID,), jnp.float32, -1.0, 1.0), -1.0, 1.0),
        "d_hidden": draw_d_hidden(jax.random.fold_in(key_list[12], 71), 0),
        "send_rows": set_ends(jax.random.randint(key_list[6], (FGROUPS, DGROUPS, PARTS_SIZE, SLOTS), 0, ROWS_DEV), jax.random.fold_in(key_list[6], 1), 0, ROWS_DEV - 1).astype(jnp.int32),
        "send_count": draw_send_count(jax.random.fold_in(key_list[12], 71), 0),
        "tile_src": draw_tile_src(jax.random.fold_in(key_list[12], 71), 0),
        "tile_dst": set_ends(jax.random.randint(key_list[9], (FGROUPS, DGROUPS, TILES), 0, LOCAL_BLOCKS), jax.random.fold_in(key_list[9], 1), 0, LOCAL_BLOCKS - 1).astype(jnp.int32),
        "tile_count": draw_tile_count(jax.random.fold_in(key_list[12], 71), 0),
        "tile_vals": draw_tile_vals(jax.random.fold_in(key_list[12], 71), 0),
    }


epsilon = 1e-05
highest = lax.Precision.HIGHEST

def reference(features, w_self, w_neigh, gain, shift, d_hidden, send_rows, send_count, tile_src, tile_dst, tile_count, tile_vals):
    stacked = features.reshape(NODES, F)
    own = jnp.dot(stacked, w_self, preferred_element_type=jnp.float32)
    neigh = jnp.dot(stacked, w_neigh, preferred_element_type=jnp.float32).astype(jnp.bfloat16).reshape(PARTS_SIZE, ROWS_DEV, HID)
    targets = send_rows.reshape(PARTS_SIZE, PARTS_SIZE, SLOTS)
    counts = send_count.reshape(PARTS_SIZE, PARTS_SIZE)
    live_slot = jnp.arange(SLOTS, dtype=jnp.int32)[None, None, :] < counts[:, :, None]
    tile_from = tile_src.reshape(PARTS_SIZE, TILES)
    tile_into = tile_dst.reshape(PARTS_SIZE, TILES)
    live_tiles = tile_count.reshape(PARTS_SIZE)
    values = tile_vals.reshape(PARTS_SIZE, TILES, TILE, TILE)
    senders = jnp.arange(PARTS_SIZE, dtype=jnp.int32)

    def aggregate(target):
        picked = neigh[senders[:, None], targets[:, target, :]]
        halo = jnp.where(live_slot[:, target, :, None], picked, jnp.zeros((), jnp.bfloat16))
        source = jnp.concatenate([neigh[target], halo.reshape(HALO_ROWS, HID)], axis=0)
        source = source.reshape(SRC_BLOCKS, TILE, HID).astype(jnp.float32)
        tiles_here = values[target].astype(jnp.float32)
        active = jnp.arange(TILES, dtype=jnp.int32) < live_tiles[target]
        products = jnp.einsum('tij,tjh->tih', tiles_here, source[tile_from[target]], precision=highest)
        placing = ((tile_into[target][None, :] == jnp.arange(LOCAL_BLOCKS, dtype=jnp.int32)[:, None]) & active[None, :]).astype(jnp.float32)
        summed = jnp.einsum('bt,tih->bih', placing, products, precision=highest).reshape(ROWS_DEV, HID)
        degree = 1.0 + jnp.dot(placing, lax.optimization_barrier(jnp.sum(tiles_here, axis=2)), precision=highest).reshape(ROWS_DEV)
        return (summed, degree)
    summed_all, degree_all = lax.map(aggregate, senders)
    degree = degree_all.reshape(NODES)
    pre = own + summed_all.reshape(NODES, HID) / degree[:, None]
    mean_pre = lax.optimization_barrier(jnp.sum(pre, axis=0)) / NODES
    variance = lax.optimization_barrier(jnp.sum(pre * pre, axis=0)) / NODES - mean_pre * mean_pre
    inverse = 1.0 / jnp.sqrt(variance + epsilon)
    normed = (pre - mean_pre) * inverse
    act = gain * normed + shift
    logistic = jax.nn.sigmoid(act)
    hidden = (act * logistic).astype(jnp.bfloat16)
    slope = d_hidden.reshape(NODES, HID).astype(jnp.float32) * logistic * (1.0 + act * (1.0 - logistic))
    shift_grad = lax.optimization_barrier(jnp.sum(slope, axis=0)) / NODES
    gain_grad = lax.optimization_barrier(jnp.sum(slope * normed, axis=0)) / NODES
    dpre = gain * inverse * (slope - shift_grad - normed * gain_grad)
    message_grad = (dpre / degree[:, None]).astype(jnp.bfloat16).reshape(PARTS_SIZE, LOCAL_BLOCKS, TILE, HID)

    def spread(running, target):
        tiles_here = values[target].astype(jnp.float32)
        active = jnp.arange(TILES, dtype=jnp.int32) < live_tiles[target]
        picked = message_grad[target][tile_into[target]].astype(jnp.float32)
        products = jnp.einsum('tij,tih->tjh', tiles_here, picked, precision=highest)
        placing = ((tile_from[target][None, :] == jnp.arange(SRC_BLOCKS, dtype=jnp.int32)[:, None]) & active[None, :]).astype(jnp.float32)
        source_grad = jnp.einsum('st,tjh->sjh', placing, products, precision=highest).reshape(SRC_BLOCKS * TILE, HID)
        running = running.at[target].add(source_grad[:ROWS_DEV])
        halo_grad = source_grad[ROWS_DEV:].astype(jnp.bfloat16)
        halo_grad = lax.optimization_barrier(halo_grad).astype(jnp.float32).reshape(PARTS_SIZE, SLOTS, HID)
        halo_grad = jnp.where(live_slot[:, target, :, None], halo_grad, jnp.zeros((), jnp.float32))
        running = running.at[senders[:, None], targets[:, target, :]].add(halo_grad)
        return (running, None)
    neigh_grad, _ = lax.scan(spread, jnp.zeros((PARTS_SIZE, ROWS_DEV, HID), jnp.float32), senders)
    out_shape = (FGROUPS, DGROUPS, ROWS_DEV, HID)
    return (hidden.reshape(out_shape), dpre.astype(jnp.bfloat16).reshape(out_shape), neigh_grad.astype(jnp.bfloat16).reshape(out_shape), gain_grad, shift_grad)
```

```python
import functools

import jax
import jax.numpy as jnp
from jax import lax
from jax.experimental import pallas as pl
from jax.experimental.pallas import tpu as pltpu
from jax.sharding import PartitionSpec as P

epsilon = 1e-05
MESH = pl.DeviceIdType.MESH
VM = pl.BlockSpec(memory_space=pltpu.VMEM)
SM = pl.BlockSpec(memory_space=pltpu.SMEM)
ANY = pl.BlockSpec(memory_space=pl.ANY)
f32 = jnp.float32
bf16 = jnp.bfloat16


def place(feat_size, dom_size):
    me_f, me_d = lax.axis_index("feat"), lax.axis_index("dom")
    me = me_f * dom_size + me_d
    total = feat_size * dom_size

    def peer_of(k):
        peer = lax.rem(me + k, total)
        return peer, (lax.div(peer, dom_size), lax.rem(peer, dom_size))

    return me_f, me_d, me, total, peer_of


def meet_all(total, peer_of):
    barrier = pltpu.get_barrier_semaphore()

    def greet(k, carry):
        _, where = peer_of(k)
        pl.semaphore_signal(barrier, inc=1, device_id=where, device_id_type=MESH)
        return carry

    lax.fori_loop(1, total, greet, 0)
    pl.semaphore_wait(barrier, total - 1)


def exchange(me, total, peer_of, source_of, target_of, send_sems, recv_sems):
    def copy_to(peer, where):
        return pltpu.make_async_remote_copy(
            src_ref=source_of(peer),
            dst_ref=target_of(me),
            send_sem=send_sems.at[peer],
            recv_sem=recv_sems.at[me],
            device_id=where,
            device_id_type=MESH,
        )

    def copy_from(peer, where):
        return pltpu.make_async_remote_copy(
            src_ref=source_of(peer),
            dst_ref=target_of(peer),
            send_sem=send_sems.at[peer],
            recv_sem=recv_sems.at[peer],
            device_id=where,
            device_id_type=MESH,
        )

    def begin():
        def start(k, carry):
            copy_to(*peer_of(k)).start()
            return carry

        lax.fori_loop(1, total, start, 0)

    def finish_recv():
        def wait(k, carry):
            copy_from(*peer_of(k)).wait_recv()
            return carry

        lax.fori_loop(1, total, wait, 0)

    def finish_send():
        def wait(k, carry):
            copy_to(*peer_of(k)).wait_send()
            return carry

        lax.fori_loop(1, total, wait, 0)

    return begin, finish_recv, finish_send


def selection(rows_ref, count_ref, node_rows):
    rows = rows_ref[0, 0]
    parts, slots = rows.shape
    counts = jnp.broadcast_to(count_ref[0], (slots, parts)).T
    live = lax.broadcasted_iota(jnp.int32, (parts, slots), 1) < counts
    wanted = jnp.where(live, rows, -1)
    nodes = lax.broadcasted_iota(jnp.int32, (parts, slots, node_rows), 2)
    picked = wanted[:, :, None] == nodes
    return jnp.where(picked, 1.0, 0.0).astype(bf16).reshape(parts * slots, node_rows)


def project_kernel(feat_size, dom_size, x_ref, ws_ref, wn_ref, rows_ref, count_ref,
                   own_ref, source_ref, xbuf, wnbuf, wsbuf, acc, pick, outgoing,
                   local_sems, near_send, near_recv, far_send, far_recv):
    me_f, me_d, me, total, peer_of = place(feat_size, dom_size)
    node_rows = x_ref.shape[2]
    slots = rows_ref.shape[3]
    mine = [
        pltpu.make_async_copy(wn_ref, wnbuf.at[me_f], local_sems.at[0]),
        pltpu.make_async_copy(x_ref.at[me_f, 0], xbuf.at[me_f], local_sems.at[1]),
        pltpu.make_async_copy(ws_ref, wsbuf.at[me_f], local_sems.at[2]),
    ]
    for copy in mine:
        copy.start()
    meet_all(total, peer_of)

    def near(kind, k):
        other = lax.rem(me_f + k, feat_size)
        source = (wn_ref, x_ref.at[other, 0], ws_ref)[kind]
        return pltpu.make_async_remote_copy(
            src_ref=source,
            dst_ref=(wnbuf, xbuf, wsbuf)[kind].at[me_f],
            send_sem=near_send.at[kind, other],
            recv_sem=near_recv.at[kind, me_f],
            device_id=(other, me_d),
            device_id_type=MESH,
        )

    def near_arrival(kind, k):
        other = lax.rem(me_f + k, feat_size)
        source = (wn_ref, x_ref.at[other, 0], ws_ref)[kind]
        return pltpu.make_async_remote_copy(
            src_ref=source,
            dst_ref=(wnbuf, xbuf, wsbuf)[kind].at[other],
            send_sem=near_send.at[kind, other],
            recv_sem=near_recv.at[kind, other],
            device_id=(other, me_d),
            device_id_type=MESH,
        )

    for kind in range(3):
        for k in range(1, feat_size):
            near(kind, k).start()
    pick[...] = selection(rows_ref, count_ref, node_rows)
    mine[0].wait()
    mine[1].wait()
    acc[...] = jnp.dot(xbuf[me_f], wnbuf[me_f], preferred_element_type=f32)
    for k in range(1, feat_size):
        near_arrival(0, k).wait_recv()
        near_arrival(1, k).wait_recv()
        other = lax.rem(me_f + k, feat_size)
        acc[...] += jnp.dot(xbuf[other], wnbuf[other], preferred_element_type=f32)
    neigh = acc[...].astype(bf16)
    source_ref[0:node_rows] = neigh
    outgoing[...] = jnp.dot(pick[...], neigh, preferred_element_type=f32).astype(bf16)

    def out_rows(peer):
        return outgoing.at[pl.ds(pl.multiple_of(peer * slots, slots), slots)]

    def in_rows(peer):
        return source_ref.at[pl.ds(pl.multiple_of(node_rows + peer * slots, slots), slots)]

    begin, finish_recv, finish_send = exchange(me, total, peer_of, out_rows, in_rows, far_send, far_recv)
    begin()
    source_ref[pl.ds(pl.multiple_of(node_rows + me * slots, slots), slots)] = outgoing[
        pl.ds(pl.multiple_of(me * slots, slots), slots)
    ]
    mine[2].wait()
    own_ref[...] = jnp.dot(xbuf[me_f], wsbuf[me_f], preferred_element_type=f32)
    for k in range(1, feat_size):
        near_arrival(2, k).wait_recv()
        other = lax.rem(me_f + k, feat_size)
        own_ref[...] += jnp.dot(xbuf[other], wsbuf[other], preferred_element_type=f32)
    for kind in range(3):
        for k in range(1, feat_size):
            near(kind, k).wait_send()
    finish_recv()
    finish_send()


def load_turns(vals_ref, vbuf, sems, turns, per_turn):
    def chunk(i):
        span = pl.ds(i * per_turn, per_turn)
        return pltpu.make_async_copy(vals_ref.at[0, 0, span], vbuf.at[span], sems.at[i])

    def start(i, carry):
        chunk(i).start()
        return carry

    lax.fori_loop(0, turns, start, 0)
    return chunk


def gather_kernel(per_turn, own_ref, source_ref, from_ref, into_ref, count_ref, vals_ref,
                  pre_ref, scale_ref, stats_ref, acc, weight, vbuf, sems):
    blocks = acc.shape[0] - 1
    tile = acc.shape[1]
    live = count_ref[0, 0]
    turns = lax.div(live + per_turn - 1, per_turn)
    chunk = load_turns(vals_ref, vbuf, sems, turns, per_turn)
    acc[...] = jnp.zeros_like(acc)
    weight[...] = jnp.zeros_like(weight)

    def turn(i, carry):
        chunk(i).wait()
        products = []
        for j in range(per_turn):
            t = i * per_turn + j
            products.append(jnp.dot(vbuf[t], source_ref[from_ref[0, 0, t]], preferred_element_type=f32))
        for j in range(per_turn):
            t = i * per_turn + j
            into = jnp.where(t < live, into_ref[0, 0, t], blocks)
            acc[into] += products[j]
            weight[into] += vbuf[t].astype(f32)
        return carry

    lax.fori_loop(0, turns, turn, 0)
    total = jnp.zeros((1, acc.shape[2]), f32)
    squares = jnp.zeros((1, acc.shape[2]), f32)
    for b in range(blocks):
        degree = 1.0 + jnp.sum(weight[b], axis=1, keepdims=True)
        inverse = 1.0 / degree
        span = slice(b * tile, (b + 1) * tile)
        pre = own_ref[span] + acc[b] * inverse
        pre_ref[span] = pre
        scale_ref[span] = jnp.broadcast_to(inverse, (tile, 128))
        total += jnp.sum(pre, axis=0, keepdims=True)
        squares += jnp.sum(pre * pre, axis=0, keepdims=True)
    stats_ref[0:1] = total
    stats_ref[1:2] = squares


def norm_kernel(feat_size, dom_size, tile, pre_ref, scale_ref, stats_ref, gain_ref, shift_ref, dh_ref,
                hidden_ref, dself_ref, mg_ref, ggrad_ref, sgrad_ref,
                normed_buf, slope_buf, first, second, local, send1, recv1, send2, recv2):
    me_f, me_d, me, total, peer_of = place(feat_size, dom_size)
    node_rows, width = pre_ref.shape
    nodes = node_rows * total
    blocks = node_rows // tile
    first[me] = stats_ref[...]
    meet_all(total, peer_of)
    begin, finish_recv, finish_send1 = exchange(
        me, total, peer_of, lambda peer: stats_ref, lambda peer: first.at[peer], send1, recv1)
    begin()
    finish_recv()
    sums = jnp.sum(first[...], axis=0)
    mean = sums[0:1] / nodes
    variance = sums[1:2] / nodes - mean * mean
    inverse = 1.0 / jnp.sqrt(variance + epsilon)
    gain = gain_ref[...].reshape(1, width)
    shift = shift_ref[...].reshape(1, width)
    slope_sum = jnp.zeros((1, width), f32)
    product_sum = jnp.zeros((1, width), f32)
    for b in range(blocks):
        span = slice(b * tile, (b + 1) * tile)
        normed = (pre_ref[span] - mean) * inverse
        act = gain * normed + shift
        logistic = jax.nn.sigmoid(act)
        hidden_ref[span] = (act * logistic).astype(bf16)
        slope = dh_ref[0, 0, span].astype(f32) * logistic * (1.0 + act * (1.0 - logistic))
        normed_buf[span] = normed
        slope_buf[span] = slope
        slope_sum += jnp.sum(slope, axis=0, keepdims=True)
        product_sum += jnp.sum(slope * normed, axis=0, keepdims=True)
    local[0:1] = slope_sum
    local[1:2] = product_sum
    second[me] = local[...]
    begin, finish_recv, finish_send2 = exchange(
        me, total, peer_of, lambda peer: local, lambda peer: second.at[peer], send2, recv2)
    begin()
    finish_recv()
    sums = jnp.sum(second[...], axis=0)
    shift_grad = sums[0:1] / nodes
    gain_grad = sums[1:2] / nodes
    sgrad_ref[...] = shift_grad
    ggrad_ref[...] = gain_grad
    factor = gain * inverse
    for b in range(blocks):
        span = slice(b * tile, (b + 1) * tile)
        dpre = factor * (slope_buf[span] - shift_grad - normed_buf[span] * gain_grad)
        dself_ref[span] = dpre.astype(bf16)
        mg_ref[b] = (dpre * scale_ref[span, 0:1]).astype(bf16)
    finish_send1()
    finish_send2()


def spread_kernel(per_turn, own_blocks, mg_ref, from_ref, into_ref, count_ref, vals_ref,
                  near_ref, halo_ref, acc, vbuf, sems):
    blocks = acc.shape[0] - 1
    live = count_ref[0, 0]
    turns = lax.div(live + per_turn - 1, per_turn)
    chunk = load_turns(vals_ref, vbuf, sems, turns, per_turn)
    acc[...] = jnp.zeros_like(acc)

    def turn(i, carry):
        chunk(i).wait()
        products = []
        for j in range(per_turn):
            t = i * per_turn + j
            products.append(lax.dot_general(
                vbuf[t], mg_ref[into_ref[0, 0, t]], (((0,), (0,)), ((), ())), preferred_element_type=f32))
        for j in range(per_turn):
            t = i * per_turn + j
            origin = jnp.where(t < live, from_ref[0, 0, t], blocks)
            acc[origin] += products[j]
        return carry

    lax.fori_loop(0, turns, turn, 0)
    near_ref[...] = acc[0:own_blocks]
    halo_ref[...] = acc[own_blocks:blocks].astype(bf16)


def return_kernel(feat_size, dom_size, near_ref, halo_ref, rows_ref, count_ref,
                  out_ref, returned, pick, send, recv):
    me_f, me_d, me, total, peer_of = place(feat_size, dom_size)
    slots = rows_ref.shape[3]
    node_rows = near_ref.shape[0]

    def rows_of(ref):
        return lambda peer: ref.at[pl.ds(pl.multiple_of(peer * slots, slots), slots)]

    returned[pl.ds(pl.multiple_of(me * slots, slots), slots)] = halo_ref[
        pl.ds(pl.multiple_of(me * slots, slots), slots)
    ]
    meet_all(total, peer_of)
    begin, finish_recv, finish_send = exchange(
        me, total, peer_of, rows_of(halo_ref), rows_of(returned), send, recv)
    begin()
    pick[...] = selection(rows_ref, count_ref, node_rows)
    finish_recv()
    added = lax.dot_general(pick[...], returned[...], (((0,), (0,)), ((), ())), preferred_element_type=f32)
    out_ref[...] = (near_ref[...] + added).astype(bf16)
    finish_send()


def shards(feat_size, dom_size, features, w_self, w_neigh, gain, shift, d_hidden, send_rows, send_count,
           tile_src, tile_dst, tile_count, tile_vals):
    node_rows, columns = features.shape[2], features.shape[3]
    width = w_self.shape[1]
    tiles, tile = tile_vals.shape[2], tile_vals.shape[3]
    parts, slots = send_rows.shape[2], send_rows.shape[3]
    own_blocks = node_rows // tile
    halo_rows = parts * slots
    blocks = (node_rows + halo_rows) // tile
    per_turn = next(n for n in (8, 4, 2, 1) if tiles % n == 0)
    turns = tiles // per_turn
    dma = pltpu.SemaphoreType.DMA
    shape = jax.ShapeDtypeStruct
    big = 60 * 1024 * 1024

    def remote(number):
        return pltpu.CompilerParams(collective_id=number, has_side_effects=True, vmem_limit_bytes=big)

    own, source = pl.pallas_call(
        functools.partial(project_kernel, feat_size, dom_size),
        out_shape=(shape((node_rows, width), f32), shape((node_rows + halo_rows, width), bf16)),
        in_specs=[ANY, ANY, ANY, VM, VM],
        out_specs=(VM, VM),
        scratch_shapes=[
            pltpu.VMEM((feat_size, node_rows, columns), bf16),
            pltpu.VMEM((feat_size, columns, width), bf16),
            pltpu.VMEM((feat_size, columns, width), bf16),
            pltpu.VMEM((node_rows, width), f32),
            pltpu.VMEM((halo_rows, node_rows), bf16),
            pltpu.VMEM((halo_rows, width), bf16),
            dma((3,)), dma((3, feat_size)), dma((3, feat_size)), dma((parts,)), dma((parts,)),
        ],
        compiler_params=remote(0),
        name="project",
    )(features, w_self, w_neigh, send_rows, send_count)
    pre, scale, stats = pl.pallas_call(
        functools.partial(gather_kernel, per_turn),
        out_shape=(shape((node_rows, width), f32), shape((node_rows, 128), f32), shape((2, width), f32)),
        in_specs=[VM, VM, SM, SM, SM, ANY],
        out_specs=(VM, VM, VM),
        scratch_shapes=[
            pltpu.VMEM((own_blocks + 1, tile, width), f32),
            pltpu.VMEM((own_blocks + 1, tile, tile), f32),
            pltpu.VMEM((tiles, tile, tile), bf16),
            dma((turns,)),
        ],
        compiler_params=pltpu.CompilerParams(vmem_limit_bytes=big),
        name="gather",
    )(own, source.reshape(blocks, tile, width), tile_src, tile_dst, tile_count, tile_vals)
    hidden, d_self, message_grad, gain_grad, shift_grad = pl.pallas_call(
        functools.partial(norm_kernel, feat_size, dom_size, tile),
        out_shape=(
            shape((node_rows, width), bf16),
            shape((node_rows, width), bf16),
            shape((own_blocks, tile, width), bf16),
            shape((1, width), f32),
            shape((1, width), f32),
        ),
        in_specs=[VM] * 6,
        out_specs=(VM,) * 5,
        scratch_shapes=[
            pltpu.VMEM((node_rows, width), f32),
            pltpu.VMEM((node_rows, width), f32),
            pltpu.VMEM((parts, 2, width), f32),
            pltpu.VMEM((parts, 2, width), f32),
            pltpu.VMEM((2, width), f32),
            dma((parts,)), dma((parts,)), dma((parts,)), dma((parts,)),
        ],
        compiler_params=remote(1),
        name="norm",
    )(pre, scale, stats, gain, shift, d_hidden)
    near, halo = pl.pallas_call(
        functools.partial(spread_kernel, per_turn, own_blocks),
        out_shape=(
            shape((own_blocks, tile, width), f32),
            shape((blocks - own_blocks, tile, width), bf16),
        ),
        in_specs=[VM, SM, SM, SM, ANY],
        out_specs=(VM, VM),
        scratch_shapes=[
            pltpu.VMEM((blocks + 1, tile, width), f32),
            pltpu.VMEM((tiles, tile, tile), bf16),
            dma((turns,)),
        ],
        compiler_params=pltpu.CompilerParams(vmem_limit_bytes=big),
        name="spread",
    )(message_grad, tile_src, tile_dst, tile_count, tile_vals)
    d_neigh = pl.pallas_call(
        functools.partial(return_kernel, feat_size, dom_size),
        out_shape=shape((node_rows, width), bf16),
        in_specs=[VM] * 4,
        out_specs=VM,
        scratch_shapes=[
            pltpu.VMEM((halo_rows, width), bf16),
            pltpu.VMEM((halo_rows, node_rows), bf16),
            dma((parts,)), dma((parts,)),
        ],
        compiler_params=remote(2),
        name="giveback",
    )(near.reshape(node_rows, width), halo.reshape(halo_rows, width), send_rows, send_count)
    out_shape = (1, 1, node_rows, width)
    return (
        hidden.reshape(out_shape),
        d_self.reshape(out_shape),
        d_neigh.reshape(out_shape),
        gain_grad.reshape(width),
        shift_grad.reshape(width),
    )


def solution(mesh):
    in_specs = (
        P(None, "dom", None, "feat"),
        P("feat", None),
        P("feat", None),
        P(),
        P(),
        P("feat", "dom", None, None),
        P("feat", "dom", None, None),
        P("feat", "dom", None),
        P("feat", "dom", None),
        P("feat", "dom", None),
        P("feat", "dom"),
        P("feat", "dom", None, None, None),
    )
    out_specs = (
        P("feat", "dom", None, None),
        P("feat", "dom", None, None),
        P("feat", "dom", None, None),
        P(),
        P(),
    )
    body = functools.partial(shards, mesh.shape["feat"], mesh.shape["dom"])
    return jax.shard_map(body, mesh=mesh, in_specs=in_specs, out_specs=out_specs, check_vma=False)
```

```python
import functools

import jax
import jax.numpy as jnp
from jax import lax
from jax.experimental import pallas as pl
from jax.experimental.pallas import tpu as pltpu
from jax.sharding import PartitionSpec as P

epsilon = 1e-05
MESH = pl.DeviceIdType.MESH
VM = pl.BlockSpec(memory_space=pltpu.VMEM)
SM = pl.BlockSpec(memory_space=pltpu.SMEM)
ANY = pl.BlockSpec(memory_space=pl.ANY)
f32 = jnp.float32
bf16 = jnp.bfloat16


def place(feat_size, dom_size):
    me_f, me_d = lax.axis_index("feat"), lax.axis_index("dom")
    me = me_f * dom_size + me_d
    total = feat_size * dom_size

    def peer_of(k):
        peer = lax.rem(me + k, total)
        return peer, (lax.div(peer, dom_size), lax.rem(peer, dom_size))

    return me_f, me_d, me, total, peer_of


def meet_all(total, peer_of):
    barrier = pltpu.get_barrier_semaphore()

    def greet(k, carry):
        _, where = peer_of(k)
        pl.semaphore_signal(barrier, inc=1, device_id=where, device_id_type=MESH)
        return carry

    lax.fori_loop(1, total, greet, 0)
    pl.semaphore_wait(barrier, total - 1)


def exchange(me, me_d, total, dom_size, peer_of, source_of, target_of, send_sems, recv_sems):
    def copy(peer, where, landing):
        return pltpu.make_async_remote_copy(
            src_ref=source_of(peer),
            dst_ref=target_of(landing),
            send_sem=send_sems.at[peer],
            recv_sem=recv_sems.at[landing],
            device_id=where,
            device_id_type=MESH,
        )

    def begin_group(group, first):
        def start(k, carry):
            spot = lax.rem(me_d + k, dom_size)
            copy(group * dom_size + spot, (group, spot), me).start()
            return carry

        lax.fori_loop(first, dom_size, start, 0)

    def begin():
        def start(k, carry):
            peer, where = peer_of(k)
            copy(peer, where, me).start()
            return carry

        lax.fori_loop(1, total, start, 0)

    def finish_recv():
        def wait(k, carry):
            peer, where = peer_of(k)
            copy(peer, where, peer).wait_recv()
            return carry

        lax.fori_loop(1, total, wait, 0)

    def finish_send():
        def wait(k, carry):
            peer, where = peer_of(k)
            copy(peer, where, me).wait_send()
            return carry

        lax.fori_loop(1, total, wait, 0)

    return begin, begin_group, finish_recv, finish_send


def selection(rows_ref, count_ref, node_rows):
    rows = rows_ref[0, 0]
    parts, slots = rows.shape
    counts = jnp.broadcast_to(count_ref[0], (slots, parts)).T
    live = lax.broadcasted_iota(jnp.int32, (parts, slots), 1) < counts
    wanted = jnp.where(live, rows, -1)
    nodes = lax.broadcasted_iota(jnp.int32, (parts, slots, node_rows), 2)
    picked = wanted[:, :, None] == nodes
    return jnp.where(picked, 1.0, 0.0).astype(bf16).reshape(parts * slots, node_rows)


def load_turns(vals_ref, vbuf, sems, turns, per_turn):
    def chunk(i):
        span = pl.ds(i * per_turn, per_turn)
        return pltpu.make_async_copy(vals_ref.at[0, 0, span], vbuf.at[span], sems.at[i])

    def start(i, carry):
        chunk(i).start()
        return carry

    lax.fori_loop(0, turns, start, 0)
    return chunk


def dense_kernel(per_turn, from_ref, into_ref, count_ref, vals_ref, hi_ref, lo_ref, scale_ref, acc, vbuf, sems):
    tile = vbuf.shape[1]
    into_blocks = hi_ref.shape[0] // tile
    from_blocks = hi_ref.shape[1] // tile
    spare = into_blocks * from_blocks
    live = count_ref[0, 0]
    turns = lax.div(live + per_turn - 1, per_turn)
    chunk = load_turns(vals_ref, vbuf, sems, turns, per_turn)
    acc[...] = jnp.zeros_like(acc)

    def turn(i, carry):
        chunk(i).wait()
        for j in range(per_turn):
            t = i * per_turn + j
            spot = into_ref[0, 0, t] * from_blocks + from_ref[0, 0, t]
            acc[jnp.where(t < live, spot, spare)] += vbuf[t].astype(f32)
        return carry

    lax.fori_loop(0, turns, turn, 0)
    for b in range(into_blocks):
        span = slice(b * tile, (b + 1) * tile)
        weight = jnp.zeros((tile, tile), f32)
        for s in range(from_blocks):
            value = acc[b * from_blocks + s]
            weight += value
            high = value.astype(bf16)
            hi_ref[span, s * tile:(s + 1) * tile] = high
            lo_ref[span, s * tile:(s + 1) * tile] = (value - high.astype(f32)).astype(bf16)
        inverse = 1.0 / (1.0 + jnp.sum(weight, axis=1, keepdims=True))
        scale_ref[span] = jnp.broadcast_to(inverse, (tile, 128))


def layer_kernel(feat_size, dom_size, tile, x_ref, ws_ref, wn_ref, rows_ref, count_ref, hi_ref, lo_ref,
                 scale_ref, gain_ref, shift_ref, dh_ref,
                 hidden_ref, dself_ref, dneigh_ref, ggrad_ref, sgrad_ref,
                 xbuf, wnbuf, wsbuf, own, summed, neigh, halo, outgoing, pick, pick_t, ah, al, ah_t, al_t,
                 mg, back_out, returned, normed_buf, slope_buf, first, second, local_a, local_b,
                 local_sems, near_send, near_recv, sib_send, sib_recv,
                 send1, recv1, send2, recv2, send3, recv3, send4, recv4):
    me_f, me_d, me, total, peer_of = place(feat_size, dom_size)
    node_rows = x_ref.shape[2]
    columns, width = wn_ref.shape
    slots = rows_ref.shape[3]
    group_rows = dom_size * slots
    halo_rows = total * slots
    nodes = node_rows * total
    half = columns // 2
    side = lax.rem(me_d, 2)
    sibling = me_d + 1 - 2 * side
    mine_rows = pl.ds(pl.multiple_of(side * half, half), half)
    other_rows = pl.ds(pl.multiple_of((1 - side) * half, half), half)
    local_copies = [
        pltpu.make_async_copy(wn_ref, wnbuf.at[me_f], local_sems.at[0]),
        pltpu.make_async_copy(x_ref.at[me_f, 0], xbuf.at[me_f], local_sems.at[1]),
        pltpu.make_async_copy(ws_ref, wsbuf.at[me_f], local_sems.at[2]),
        pltpu.make_async_copy(hi_ref, ah, local_sems.at[3]),
        pltpu.make_async_copy(lo_ref, al, local_sems.at[4]),
    ]
    for copy in local_copies:
        copy.start()
    meet_all(total, peer_of)

    def near(kind, k, arriving):
        other = lax.rem(me_f + k, feat_size)
        landing = other if arriving else me_f
        if kind == 1:
            source, target = x_ref.at[other, 0], xbuf.at[landing]
        else:
            source = (wn_ref, None, ws_ref)[kind].at[mine_rows]
            target = (wnbuf, None, wsbuf)[kind].at[landing, mine_rows]
        return pltpu.make_async_remote_copy(
            src_ref=source,
            dst_ref=target,
            send_sem=near_send.at[kind, other],
            recv_sem=near_recv.at[kind, landing],
            device_id=(other, me_d),
            device_id_type=MESH,
        )

    def passed(kind, k, arriving):
        other = lax.rem(me_f + k, feat_size)
        buffer = (wnbuf, None, wsbuf)[kind]
        return pltpu.make_async_remote_copy(
            src_ref=buffer.at[other, mine_rows],
            dst_ref=buffer.at[other, other_rows if arriving else mine_rows],
            send_sem=sib_send.at[kind, other],
            recv_sem=sib_recv.at[kind, other],
            device_id=(me_f, sibling),
            device_id_type=MESH,
        )

    for kind in range(3):
        for k in range(1, feat_size):
            near(kind, k, False).start()
    pick[...] = selection(rows_ref, count_ref, node_rows)
    for k in range(1, feat_size):
        near(0, k, True).wait_recv()
        passed(0, k, False).start()
    for copy in local_copies:
        copy.wait()

    def turn_block(s, carry):
        lanes = pl.ds(pl.multiple_of(s * tile, tile), tile)
        ah_t[lanes, :] = ah[:, lanes].T
        al_t[lanes, :] = al[:, lanes].T
        return carry

    lax.fori_loop(0, (node_rows + halo_rows) // tile, turn_block, 0)
    summed[...] = jnp.dot(xbuf[me_f], wnbuf[me_f], preferred_element_type=f32)
    for k in range(1, feat_size):
        passed(0, k, True).wait_recv()
        near(1, k, True).wait_recv()
        other = lax.rem(me_f + k, feat_size)
        summed[...] += jnp.dot(xbuf[other], wnbuf[other], preferred_element_type=f32)
    neigh[...] = summed[...].astype(bf16)

    def slots_of(ref):
        return lambda peer: ref.at[pl.ds(pl.multiple_of(peer * slots, slots), slots)]

    mine = pl.ds(pl.multiple_of(me * slots, slots), slots)
    _, begin_group, finish_recv, finish_send1 = exchange(
        me, me_d, total, dom_size, peer_of, slots_of(outgoing), slots_of(halo), send1, recv1)
    for i in range(feat_size):
        group = lax.rem(me_f + i, feat_size)
        span = pl.ds(pl.multiple_of(group * group_rows, group_rows), group_rows)
        outgoing[span] = jnp.dot(pick[span], neigh[...], preferred_element_type=f32).astype(bf16)
        begin_group(group, 1 if i == 0 else 0)
    halo[mine] = outgoing[mine]
    for k in range(1, feat_size):
        near(2, k, True).wait_recv()
        passed(2, k, False).start()
    summed[...] = jnp.dot(ah[:, 0:node_rows], neigh[...], preferred_element_type=f32)
    summed[...] += jnp.dot(al[:, 0:node_rows], neigh[...], preferred_element_type=f32)
    own[...] = jnp.dot(xbuf[me_f], wsbuf[me_f], preferred_element_type=f32)
    for k in range(1, feat_size):
        passed(2, k, True).wait_recv()
        other = lax.rem(me_f + k, feat_size)
        own[...] += jnp.dot(xbuf[other], wsbuf[other], preferred_element_type=f32)

    def turn_pick(s, carry):
        rows = pl.ds(pl.multiple_of(s * tile, tile), tile)
        pick_t[:, rows] = pick[rows, :].T
        return carry

    lax.fori_loop(0, halo_rows // tile, turn_pick, 0)
    finish_recv()
    summed[...] += jnp.dot(ah[:, node_rows:], halo[...], preferred_element_type=f32)
    summed[...] += jnp.dot(al[:, node_rows:], halo[...], preferred_element_type=f32)
    blocks = node_rows // tile
    col_sum = jnp.zeros((1, width), f32)
    col_square = jnp.zeros((1, width), f32)
    for b in range(blocks):
        span = slice(b * tile, (b + 1) * tile)
        pre = own[span] + summed[span] * scale_ref[span, 0:1]
        own[span] = pre
        col_sum += jnp.sum(pre, axis=0, keepdims=True)
        col_square += jnp.sum(pre * pre, axis=0, keepdims=True)
    local_a[0:1] = col_sum
    local_a[1:2] = col_square
    first[me] = local_a[...]
    begin, _, finish_recv, finish_send2 = exchange(
        me, me_d, total, dom_size, peer_of, lambda peer: local_a, lambda peer: first.at[peer], send2, recv2)
    begin()
    finish_recv()
    sums = jnp.sum(first[...], axis=0)
    mean = sums[0:1] / nodes
    variance = sums[1:2] / nodes - mean * mean
    inverse = 1.0 / jnp.sqrt(variance + epsilon)
    gain = gain_ref[...].reshape(1, width)
    shift = shift_ref[...].reshape(1, width)
    slope_sum = jnp.zeros((1, width), f32)
    product_sum = jnp.zeros((1, width), f32)
    for b in range(blocks):
        span = slice(b * tile, (b + 1) * tile)
        normed = (own[span] - mean) * inverse
        act = gain * normed + shift
        logistic = jax.nn.sigmoid(act)
        hidden_ref[span] = (act * logistic).astype(bf16)
        slope = dh_ref[0, 0, span].astype(f32) * logistic * (1.0 + act * (1.0 - logistic))
        normed_buf[span] = normed
        slope_buf[span] = slope
        slope_sum += jnp.sum(slope, axis=0, keepdims=True)
        product_sum += jnp.sum(slope * normed, axis=0, keepdims=True)
    local_b[0:1] = slope_sum
    local_b[1:2] = product_sum
    second[me] = local_b[...]
    begin, _, finish_recv, finish_send3 = exchange(
        me, me_d, total, dom_size, peer_of, lambda peer: local_b, lambda peer: second.at[peer], send3, recv3)
    begin()
    finish_recv()
    sums = jnp.sum(second[...], axis=0)
    shift_grad = sums[0:1] / nodes
    gain_grad = sums[1:2] / nodes
    sgrad_ref[...] = shift_grad
    ggrad_ref[...] = gain_grad
    factor = gain * inverse
    for b in range(blocks):
        span = slice(b * tile, (b + 1) * tile)
        dpre = factor * (slope_buf[span] - shift_grad - normed_buf[span] * gain_grad)
        dself_ref[span] = dpre.astype(bf16)
        mg[span] = (dpre * scale_ref[span, 0:1]).astype(bf16)
    _, begin_group, finish_recv, finish_send4 = exchange(
        me, me_d, total, dom_size, peer_of, slots_of(back_out), slots_of(returned), send4, recv4)
    for i in range(feat_size):
        group = lax.rem(me_f + i, feat_size)
        span = pl.ds(pl.multiple_of(group * group_rows, group_rows), group_rows)
        edges = pl.ds(pl.multiple_of(node_rows + group * group_rows, tile), group_rows)
        back_out[span] = (
            jnp.dot(ah_t[edges], mg[...], preferred_element_type=f32)
            + jnp.dot(al_t[edges], mg[...], preferred_element_type=f32)
        ).astype(bf16)
        begin_group(group, 1 if i == 0 else 0)
    returned[mine] = back_out[mine]
    summed[...] = jnp.dot(ah_t[0:node_rows], mg[...], preferred_element_type=f32)
    summed[...] += jnp.dot(al_t[0:node_rows], mg[...], preferred_element_type=f32)
    for k in range(1, feat_size):
        for kind in range(3):
            near(kind, k, False).wait_send()
        passed(0, k, False).wait_send()
        passed(2, k, False).wait_send()
    finish_send1()
    finish_send2()
    finish_send3()
    finish_recv()
    added = jnp.dot(pick_t[...], returned[...], preferred_element_type=f32)
    dneigh_ref[...] = (summed[...] + added).astype(bf16)
    finish_send4()


def shards(feat_size, dom_size, features, w_self, w_neigh, gain, shift, d_hidden, send_rows, send_count,
           tile_src, tile_dst, tile_count, tile_vals):
    node_rows, columns = features.shape[2], features.shape[3]
    width = w_self.shape[1]
    tiles, tile = tile_vals.shape[2], tile_vals.shape[3]
    parts, slots = send_rows.shape[2], send_rows.shape[3]
    own_blocks = node_rows // tile
    halo_rows = parts * slots
    all_rows = node_rows + halo_rows
    blocks = all_rows // tile
    per_turn = next(n for n in (8, 4, 2, 1) if tiles % n == 0)
    dma = pltpu.SemaphoreType.DMA
    shape = jax.ShapeDtypeStruct
    big = 60 * 1024 * 1024
    high, low, scale = pl.pallas_call(
        functools.partial(dense_kernel, per_turn),
        out_shape=(
            shape((node_rows, all_rows), bf16),
            shape((node_rows, all_rows), bf16),
            shape((node_rows, 128), f32),
        ),
        in_specs=[SM, SM, SM, ANY],
        out_specs=(VM, VM, VM),
        scratch_shapes=[
            pltpu.VMEM((own_blocks * blocks + 1, tile, tile), f32),
            pltpu.VMEM((tiles, tile, tile), bf16),
            dma((tiles // per_turn,)),
        ],
        compiler_params=pltpu.CompilerParams(vmem_limit_bytes=big),
        name="dense",
    )(tile_src, tile_dst, tile_count, tile_vals)
    hidden, d_self, d_neigh, gain_grad, shift_grad = pl.pallas_call(
        functools.partial(layer_kernel, feat_size, dom_size, tile),
        out_shape=(
            shape((node_rows, width), bf16),
            shape((node_rows, width), bf16),
            shape((node_rows, width), bf16),
            shape((1, width), f32),
            shape((1, width), f32),
        ),
        in_specs=[ANY, ANY, ANY, VM, VM, ANY, ANY, VM, VM, VM, VM],
        out_specs=(VM,) * 5,
        scratch_shapes=[
            pltpu.VMEM((feat_size, node_rows, columns), bf16),
            pltpu.VMEM((feat_size, columns, width), bf16),
            pltpu.VMEM((feat_size, columns, width), bf16),
            pltpu.VMEM((node_rows, width), f32),
            pltpu.VMEM((node_rows, width), f32),
            pltpu.VMEM((node_rows, width), bf16),
            pltpu.VMEM((halo_rows, width), bf16),
            pltpu.VMEM((halo_rows, width), bf16),
            pltpu.VMEM((halo_rows, node_rows), bf16),
            pltpu.VMEM((node_rows, halo_rows), bf16),
            pltpu.VMEM((node_rows, all_rows), bf16),
            pltpu.VMEM((node_rows, all_rows), bf16),
            pltpu.VMEM((all_rows, node_rows), bf16),
            pltpu.VMEM((all_rows, node_rows), bf16),
            pltpu.VMEM((node_rows, width), bf16),
            pltpu.VMEM((halo_rows, width), bf16),
            pltpu.VMEM((halo_rows, width), bf16),
            pltpu.VMEM((node_rows, width), f32),
            pltpu.VMEM((node_rows, width), f32),
            pltpu.VMEM((parts, 2, width), f32),
            pltpu.VMEM((parts, 2, width), f32),
            pltpu.VMEM((2, width), f32),
            pltpu.VMEM((2, width), f32),
            dma((5,)), dma((3, feat_size)), dma((3, feat_size)), dma((3, feat_size)), dma((3, feat_size)),
        ] + [dma((parts,)) for _ in range(8)],
        compiler_params=pltpu.CompilerParams(collective_id=0, has_side_effects=True, vmem_limit_bytes=big),
        name="layer",
    )(features, w_self, w_neigh, send_rows, send_count, high, low, scale, gain, shift, d_hidden)
    out_shape = (1, 1, node_rows, width)
    return (
        hidden.reshape(out_shape),
        d_self.reshape(out_shape),
        d_neigh.reshape(out_shape),
        gain_grad.reshape(width),
        shift_grad.reshape(width),
    )


def solution(mesh):
    in_specs = (
        P(None, "dom", None, "feat"),
        P("feat", None),
        P("feat", None),
        P(),
        P(),
        P("feat", "dom", None, None),
        P("feat", "dom", None, None),
        P("feat", "dom", None),
        P("feat", "dom", None),
        P("feat", "dom", None),
        P("feat", "dom"),
        P("feat", "dom", None, None, None),
    )
    out_specs = (
        P("feat", "dom", None, None),
        P("feat", "dom", None, None),
        P("feat", "dom", None, None),
        P(),
        P(),
    )
    body = functools.partial(shards, mesh.shape["feat"], mesh.shape["dom"])
    return jax.shard_map(body, mesh=mesh, in_specs=in_specs, out_specs=out_specs, check_vma=False)
```

```python
import functools

import jax
import jax.numpy as jnp
from jax import lax
from jax.experimental import pallas as pl
from jax.experimental.pallas import tpu as pltpu
from jax.sharding import PartitionSpec as P

epsilon = 1e-05
MESH = pl.DeviceIdType.MESH
VM = pl.BlockSpec(memory_space=pltpu.VMEM)
SM = pl.BlockSpec(memory_space=pltpu.SMEM)
ANY = pl.BlockSpec(memory_space=pl.ANY)
f32 = jnp.float32
bf16 = jnp.bfloat16


def place(feat_size, dom_size):
    me_f, me_d = lax.axis_index("feat"), lax.axis_index("dom")
    me = me_f * dom_size + me_d
    total = feat_size * dom_size

    def peer_of(k):
        peer = lax.rem(me + k, total)
        return peer, (lax.div(peer, dom_size), lax.rem(peer, dom_size))

    return me_f, me_d, me, total, peer_of


def meet_all(total, peer_of, while_waiting):
    barrier = pltpu.get_barrier_semaphore()

    def greet(k, carry):
        _, where = peer_of(k)
        pl.semaphore_signal(barrier, inc=1, device_id=where, device_id_type=MESH)
        return carry

    lax.fori_loop(1, total, greet, 0)
    while_waiting()
    pl.semaphore_wait(barrier, total - 1)


def exchange(me, me_d, total, dom_size, peer_of, source_of, target_of, send_sems, recv_sems):
    def copy(peer, where, landing):
        return pltpu.make_async_remote_copy(
            src_ref=source_of(peer),
            dst_ref=target_of(landing),
            send_sem=send_sems.at[peer],
            recv_sem=recv_sems.at[landing],
            device_id=where,
            device_id_type=MESH,
        )

    def begin_group(group, first):
        def start(k, carry):
            spot = lax.rem(me_d + k, dom_size)
            copy(group * dom_size + spot, (group, spot), me).start()
            return carry

        lax.fori_loop(first, dom_size, start, 0)

    def begin():
        def start(k, carry):
            peer, where = peer_of(k)
            copy(peer, where, me).start()
            return carry

        lax.fori_loop(1, total, start, 0)

    def finish_recv():
        def wait(k, carry):
            peer, where = peer_of(k)
            copy(peer, where, peer).wait_recv()
            return carry

        lax.fori_loop(1, total, wait, 0)

    def finish_send():
        def wait(k, carry):
            peer, where = peer_of(k)
            copy(peer, where, me).wait_send()
            return carry

        lax.fori_loop(1, total, wait, 0)

    return begin, begin_group, finish_recv, finish_send


def selection(rows_ref, count_ref, node_rows):
    rows = rows_ref[0, 0]
    parts, slots = rows.shape
    counts = jnp.broadcast_to(count_ref[0], (slots, parts)).T
    live = lax.broadcasted_iota(jnp.int32, (parts, slots), 1) < counts
    wanted = jnp.where(live, rows, -1)
    nodes = lax.broadcasted_iota(jnp.int32, (parts, slots, node_rows), 2)
    picked = wanted[:, :, None] == nodes
    return jnp.where(picked, 1.0, 0.0).astype(bf16).reshape(parts * slots, node_rows)


def load_turns(vals_ref, vbuf, sems, turns, per_turn):
    def chunk(i):
        span = pl.ds(i * per_turn, per_turn)
        return pltpu.make_async_copy(vals_ref.at[0, 0, span], vbuf.at[span], sems.at[i])

    def start(i, carry):
        chunk(i).start()
        return carry

    lax.fori_loop(0, turns, start, 0)
    return chunk


def dense_kernel(per_turn, from_ref, into_ref, count_ref, vals_ref, hi_ref, lo_ref, scale_ref, acc, vbuf, sems):
    tile = vbuf.shape[1]
    into_blocks = hi_ref.shape[0] // tile
    from_blocks = hi_ref.shape[1] // tile
    spare = into_blocks * from_blocks
    live = count_ref[0, 0]
    turns = lax.div(live + per_turn - 1, per_turn)
    chunk = load_turns(vals_ref, vbuf, sems, turns, per_turn)
    acc[...] = jnp.zeros_like(acc)

    def turn(i, carry):
        chunk(i).wait()
        for j in range(per_turn):
            t = i * per_turn + j
            spot = into_ref[0, 0, t] * from_blocks + from_ref[0, 0, t]
            acc[jnp.where(t < live, spot, spare)] += vbuf[t].astype(f32)
        return carry

    lax.fori_loop(0, turns, turn, 0)
    for b in range(into_blocks):
        span = slice(b * tile, (b + 1) * tile)
        weight = jnp.zeros((tile, tile), f32)
        for s in range(from_blocks):
            value = acc[b * from_blocks + s]
            weight += value
            high = value.astype(bf16)
            hi_ref[span, s * tile:(s + 1) * tile] = high
            lo_ref[span, s * tile:(s + 1) * tile] = (value - high.astype(f32)).astype(bf16)
        inverse = 1.0 / (1.0 + jnp.sum(weight, axis=1, keepdims=True))
        scale_ref[span] = jnp.broadcast_to(inverse, (tile, 128))


def layer_kernel(feat_size, dom_size, tile, x_ref, ws_ref, wn_ref, rows_ref, count_ref, hi_ref, lo_ref,
                 scale_ref, gain_ref, shift_ref, dh_ref,
                 hidden_ref, dself_ref, dneigh_ref, ggrad_ref, sgrad_ref,
                 xbuf, wnbuf, wsbuf, own, summed, neigh, halo, outgoing, pick, pick_t, ah, al, ah_t, al_t,
                 mg, back_out, returned, normed_buf, slope_buf, first, second, local_a, local_b,
                 local_sems, near_send, near_recv, sib_send, sib_recv,
                 send1, recv1, send2, recv2, send3, recv3, send4, recv4):
    me_f, me_d, me, total, peer_of = place(feat_size, dom_size)
    node_rows = x_ref.shape[2]
    columns, width = wn_ref.shape
    slots = rows_ref.shape[3]
    group_rows = dom_size * slots
    halo_rows = total * slots
    nodes = node_rows * total
    half = columns // 2
    side = lax.rem(me_d, 2)
    sibling = me_d + 1 - 2 * side
    mine_rows = pl.ds(pl.multiple_of(side * half, half), half)
    other_rows = pl.ds(pl.multiple_of((1 - side) * half, half), half)
    local_copies = [
        pltpu.make_async_copy(wn_ref, wnbuf.at[me_f], local_sems.at[0]),
        pltpu.make_async_copy(x_ref.at[me_f, 0], xbuf.at[me_f], local_sems.at[1]),
        pltpu.make_async_copy(ws_ref, wsbuf.at[me_f], local_sems.at[2]),
        pltpu.make_async_copy(hi_ref, ah, local_sems.at[3]),
        pltpu.make_async_copy(lo_ref, al, local_sems.at[4]),
    ]
    for copy in local_copies:
        copy.start()

    def build_pick():
        pick[...] = selection(rows_ref, count_ref, node_rows)

    meet_all(total, peer_of, build_pick)

    def near(kind, k, arriving):
        other = lax.rem(me_f + k, feat_size)
        landing = other if arriving else me_f
        if kind == 1:
            source, target = x_ref.at[other, 0], xbuf.at[landing]
        else:
            source = (wn_ref, None, ws_ref)[kind].at[mine_rows]
            target = (wnbuf, None, wsbuf)[kind].at[landing, mine_rows]
        return pltpu.make_async_remote_copy(
            src_ref=source,
            dst_ref=target,
            send_sem=near_send.at[kind, other],
            recv_sem=near_recv.at[kind, landing],
            device_id=(other, me_d),
            device_id_type=MESH,
        )

    def passed(kind, k, arriving):
        other = lax.rem(me_f + k, feat_size)
        buffer = (wnbuf, None, wsbuf)[kind]
        return pltpu.make_async_remote_copy(
            src_ref=buffer.at[other, mine_rows],
            dst_ref=buffer.at[other, other_rows if arriving else mine_rows],
            send_sem=sib_send.at[kind, other],
            recv_sem=sib_recv.at[kind, other],
            device_id=(me_f, sibling),
            device_id_type=MESH,
        )

    for kind in range(3):
        for k in range(1, feat_size):
            near(kind, k, False).start()
    for k in range(1, feat_size):
        near(0, k, True).wait_recv()
        passed(0, k, False).start()
    for copy in local_copies:
        copy.wait()

    def turn_block(s, carry):
        lanes = pl.ds(pl.multiple_of(s * tile, tile), tile)
        ah_t[lanes, :] = ah[:, lanes].T
        al_t[lanes, :] = al[:, lanes].T
        return carry

    lax.fori_loop(0, (node_rows + halo_rows) // tile, turn_block, 0)
    summed[...] = jnp.dot(xbuf[me_f], wnbuf[me_f], preferred_element_type=f32)
    for k in range(1, feat_size):
        passed(0, k, True).wait_recv()
        near(1, k, True).wait_recv()
        other = lax.rem(me_f + k, feat_size)
        summed[...] += jnp.dot(xbuf[other], wnbuf[other], preferred_element_type=f32)
    neigh[...] = summed[...].astype(bf16)

    def slots_of(ref):
        return lambda peer: ref.at[pl.ds(pl.multiple_of(peer * slots, slots), slots)]

    mine = pl.ds(pl.multiple_of(me * slots, slots), slots)
    _, begin_group, finish_recv, finish_send1 = exchange(
        me, me_d, total, dom_size, peer_of, slots_of(outgoing), slots_of(halo), send1, recv1)
    for i in range(feat_size):
        group = lax.rem(me_f + i, feat_size)
        span = pl.ds(pl.multiple_of(group * group_rows, group_rows), group_rows)
        outgoing[span] = jnp.dot(pick[span], neigh[...], preferred_element_type=f32).astype(bf16)
        begin_group(group, 1 if i == 0 else 0)
    halo[mine] = outgoing[mine]
    for k in range(1, feat_size):
        near(2, k, True).wait_recv()
        passed(2, k, False).start()
    summed[...] = jnp.dot(ah[:, 0:node_rows], neigh[...], preferred_element_type=f32)
    summed[...] += jnp.dot(al[:, 0:node_rows], neigh[...], preferred_element_type=f32)
    own[...] = jnp.dot(xbuf[me_f], wsbuf[me_f], preferred_element_type=f32)
    for k in range(1, feat_size):
        passed(2, k, True).wait_recv()
        other = lax.rem(me_f + k, feat_size)
        own[...] += jnp.dot(xbuf[other], wsbuf[other], preferred_element_type=f32)

    def turn_pick(s, carry):
        rows = pl.ds(pl.multiple_of(s * tile, tile), tile)
        pick_t[:, rows] = pick[rows, :].T
        return carry

    lax.fori_loop(0, halo_rows // tile, turn_pick, 0)
    finish_recv()
    summed[...] += jnp.dot(ah[:, node_rows:], halo[...], preferred_element_type=f32)
    summed[...] += jnp.dot(al[:, node_rows:], halo[...], preferred_element_type=f32)
    blocks = node_rows // tile
    col_sum = jnp.zeros((1, width), f32)
    col_square = jnp.zeros((1, width), f32)
    for b in range(blocks):
        span = slice(b * tile, (b + 1) * tile)
        pre = own[span] + summed[span] * scale_ref[span, 0:1]
        own[span] = pre
        col_sum += jnp.sum(pre, axis=0, keepdims=True)
        col_square += jnp.sum(pre * pre, axis=0, keepdims=True)
    local_a[0:1] = col_sum
    local_a[1:2] = col_square
    first[me] = local_a[...]
    begin, _, finish_recv, finish_send2 = exchange(
        me, me_d, total, dom_size, peer_of, lambda peer: local_a, lambda peer: first.at[peer], send2, recv2)
    begin()
    finish_recv()
    sums = jnp.sum(first[...], axis=0)
    mean = sums[0:1] / nodes
    variance = sums[1:2] / nodes - mean * mean
    inverse = 1.0 / jnp.sqrt(variance + epsilon)
    gain = gain_ref[...].reshape(1, width)
    shift = shift_ref[...].reshape(1, width)
    slope_sum = jnp.zeros((1, width), f32)
    product_sum = jnp.zeros((1, width), f32)
    for b in range(blocks):
        span = slice(b * tile, (b + 1) * tile)
        normed = (own[span] - mean) * inverse
        act = gain * normed + shift
        logistic = jax.nn.sigmoid(act)
        hidden_ref[span] = (act * logistic).astype(bf16)
        slope = dh_ref[0, 0, span].astype(f32) * logistic * (1.0 + act * (1.0 - logistic))
        normed_buf[span] = normed
        slope_buf[span] = slope
        slope_sum += jnp.sum(slope, axis=0, keepdims=True)
        product_sum += jnp.sum(slope * normed, axis=0, keepdims=True)
    local_b[0:1] = slope_sum
    local_b[1:2] = product_sum
    second[me] = local_b[...]
    begin, _, finish_recv, finish_send3 = exchange(
        me, me_d, total, dom_size, peer_of, lambda peer: local_b, lambda peer: second.at[peer], send3, recv3)
    begin()
    finish_recv()
    sums = jnp.sum(second[...], axis=0)
    shift_grad = sums[0:1] / nodes
    gain_grad = sums[1:2] / nodes
    sgrad_ref[...] = shift_grad
    ggrad_ref[...] = gain_grad
    factor = gain * inverse
    for b in range(blocks):
        span = slice(b * tile, (b + 1) * tile)
        dpre = factor * (slope_buf[span] - shift_grad - normed_buf[span] * gain_grad)
        dself_ref[span] = dpre.astype(bf16)
        mg[span] = (dpre * scale_ref[span, 0:1]).astype(bf16)
    _, begin_group, finish_recv, finish_send4 = exchange(
        me, me_d, total, dom_size, peer_of, slots_of(back_out), slots_of(returned), send4, recv4)
    for i in range(feat_size):
        group = lax.rem(me_f + i, feat_size)
        span = pl.ds(pl.multiple_of(group * group_rows, group_rows), group_rows)
        edges = pl.ds(pl.multiple_of(node_rows + group * group_rows, tile), group_rows)
        back_out[span] = (
            jnp.dot(ah_t[edges], mg[...], preferred_element_type=f32)
            + jnp.dot(al_t[edges], mg[...], preferred_element_type=f32)
        ).astype(bf16)
        begin_group(group, 1 if i == 0 else 0)
    returned[mine] = back_out[mine]
    summed[...] = jnp.dot(ah_t[0:node_rows], mg[...], preferred_element_type=f32)
    summed[...] += jnp.dot(al_t[0:node_rows], mg[...], preferred_element_type=f32)
    for k in range(1, feat_size):
        for kind in range(3):
            near(kind, k, False).wait_send()
        passed(0, k, False).wait_send()
        passed(2, k, False).wait_send()
    finish_send1()
    finish_send2()
    finish_send3()
    finish_recv()
    added = jnp.dot(pick_t[...], returned[...], preferred_element_type=f32)
    dneigh_ref[...] = (summed[...] + added).astype(bf16)
    finish_send4()


def finish_kernel(*refs):
    count = len(refs) // 2
    for source, target in zip(refs[:count], refs[count:]):
        target[...] = source[...].reshape(target.shape)


def shards(feat_size, dom_size, features, w_self, w_neigh, gain, shift, d_hidden, send_rows, send_count,
           tile_src, tile_dst, tile_count, tile_vals):
    node_rows, columns = features.shape[2], features.shape[3]
    width = w_self.shape[1]
    tiles, tile = tile_vals.shape[2], tile_vals.shape[3]
    parts, slots = send_rows.shape[2], send_rows.shape[3]
    own_blocks = node_rows // tile
    halo_rows = parts * slots
    all_rows = node_rows + halo_rows
    blocks = all_rows // tile
    per_turn = next(n for n in (8, 4, 2, 1) if tiles % n == 0)
    dma = pltpu.SemaphoreType.DMA
    shape = jax.ShapeDtypeStruct
    big = 60 * 1024 * 1024
    high, low, scale = pl.pallas_call(
        functools.partial(dense_kernel, per_turn),
        out_shape=(
            shape((node_rows, all_rows), bf16),
            shape((node_rows, all_rows), bf16),
            shape((node_rows, 128), f32),
        ),
        in_specs=[SM, SM, SM, ANY],
        out_specs=(VM, VM, VM),
        scratch_shapes=[
            pltpu.VMEM((own_blocks * blocks + 1, tile, tile), f32),
            pltpu.VMEM((tiles, tile, tile), bf16),
            dma((tiles // per_turn,)),
        ],
        compiler_params=pltpu.CompilerParams(vmem_limit_bytes=big),
        name="dense",
    )(tile_src, tile_dst, tile_count, tile_vals)
    hidden, d_self, d_neigh, gain_grad, shift_grad = pl.pallas_call(
        functools.partial(layer_kernel, feat_size, dom_size, tile),
        out_shape=(
            shape((node_rows, width), bf16),
            shape((node_rows, width), bf16),
            shape((node_rows, width), bf16),
            shape((1, width), f32),
            shape((1, width), f32),
        ),
        in_specs=[ANY, ANY, ANY, VM, VM, ANY, ANY, VM, VM, VM, VM],
        out_specs=(VM,) * 5,
        scratch_shapes=[
            pltpu.VMEM((feat_size, node_rows, columns), bf16),
            pltpu.VMEM((feat_size, columns, width), bf16),
            pltpu.VMEM((feat_size, columns, width), bf16),
            pltpu.VMEM((node_rows, width), f32),
            pltpu.VMEM((node_rows, width), f32),
            pltpu.VMEM((node_rows, width), bf16),
            pltpu.VMEM((halo_rows, width), bf16),
            pltpu.VMEM((halo_rows, width), bf16),
            pltpu.VMEM((halo_rows, node_rows), bf16),
            pltpu.VMEM((node_rows, halo_rows), bf16),
            pltpu.VMEM((node_rows, all_rows), bf16),
            pltpu.VMEM((node_rows, all_rows), bf16),
            pltpu.VMEM((all_rows, node_rows), bf16),
            pltpu.VMEM((all_rows, node_rows), bf16),
            pltpu.VMEM((node_rows, width), bf16),
            pltpu.VMEM((halo_rows, width), bf16),
            pltpu.VMEM((halo_rows, width), bf16),
            pltpu.VMEM((node_rows, width), f32),
            pltpu.VMEM((node_rows, width), f32),
            pltpu.VMEM((parts, 2, width), f32),
            pltpu.VMEM((parts, 2, width), f32),
            pltpu.VMEM((2, width), f32),
            pltpu.VMEM((2, width), f32),
            dma((5,)), dma((3, feat_size)), dma((3, feat_size)), dma((3, feat_size)), dma((3, feat_size)),
        ] + [dma((parts,)) for _ in range(8)],
        compiler_params=pltpu.CompilerParams(collective_id=0, has_side_effects=True, vmem_limit_bytes=big),
        name="layer",
    )(features, w_self, w_neigh, send_rows, send_count, high, low, scale, gain, shift, d_hidden)
    out_shape = (1, 1, node_rows, width)
    return pl.pallas_call(
        finish_kernel,
        out_shape=(shape(out_shape, bf16),) * 3 + (shape((width,), f32),) * 2,
        in_specs=[VM] * 5,
        out_specs=(VM,) * 5,
        name="finish",
    )(hidden, d_self, d_neigh, gain_grad, shift_grad)


def solution(mesh):
    in_specs = (
        P(None, "dom", None, "feat"),
        P("feat", None),
        P("feat", None),
        P(),
        P(),
        P("feat", "dom", None, None),
        P("feat", "dom", None, None),
        P("feat", "dom", None),
        P("feat", "dom", None),
        P("feat", "dom", None),
        P("feat", "dom"),
        P("feat", "dom", None, None, None),
    )
    out_specs = (
        P("feat", "dom", None, None),
        P("feat", "dom", None, None),
        P("feat", "dom", None, None),
        P(),
        P(),
    )
    body = functools.partial(shards, mesh.shape["feat"], mesh.shape["dom"])
    return jax.shard_map(body, mesh=mesh, in_specs=in_specs, out_specs=out_specs, check_vma=False)
```

```python
import functools

import jax
import jax.numpy as jnp
from jax import lax
from jax.experimental import pallas as pl
from jax.experimental.pallas import tpu as pltpu
from jax.sharding import PartitionSpec as P

epsilon = 1e-05
MESH = pl.DeviceIdType.MESH
VM = pl.BlockSpec(memory_space=pltpu.VMEM)
SM = pl.BlockSpec(memory_space=pltpu.SMEM)
ANY = pl.BlockSpec(memory_space=pl.ANY)
f32 = jnp.float32
bf16 = jnp.bfloat16


def place(feat_size, dom_size):
    me_f, me_d = lax.axis_index("feat"), lax.axis_index("dom")
    me = me_f * dom_size + me_d
    total = feat_size * dom_size

    def peer_of(k):
        peer = lax.rem(me + k, total)
        return peer, (lax.div(peer, dom_size), lax.rem(peer, dom_size))

    return me_f, me_d, me, total, peer_of


def meet_all(total, peer_of, while_waiting):
    barrier = pltpu.get_barrier_semaphore()

    def greet(k, carry):
        _, where = peer_of(k)
        pl.semaphore_signal(barrier, inc=1, device_id=where, device_id_type=MESH)
        return carry

    lax.fori_loop(1, total, greet, 0)
    while_waiting()
    pl.semaphore_wait(barrier, total - 1)


def exchange(me, me_d, total, dom_size, peer_of, source_of, target_of, send_sems, recv_sems):
    def copy(peer, where, landing):
        return pltpu.make_async_remote_copy(
            src_ref=source_of(peer),
            dst_ref=target_of(landing),
            send_sem=send_sems.at[peer],
            recv_sem=recv_sems.at[landing],
            device_id=where,
            device_id_type=MESH,
        )

    def begin_group(group, first):
        def start(k, carry):
            spot = lax.rem(me_d + k, dom_size)
            copy(group * dom_size + spot, (group, spot), me).start()
            return carry

        lax.fori_loop(first, dom_size, start, 0)

    def begin():
        def start(k, carry):
            peer, where = peer_of(k)
            copy(peer, where, me).start()
            return carry

        lax.fori_loop(1, total, start, 0)

    def finish_recv():
        def wait(k, carry):
            peer, where = peer_of(k)
            copy(peer, where, peer).wait_recv()
            return carry

        lax.fori_loop(1, total, wait, 0)

    def finish_send():
        def wait(k, carry):
            peer, where = peer_of(k)
            copy(peer, where, me).wait_send()
            return carry

        lax.fori_loop(1, total, wait, 0)

    return begin, begin_group, finish_recv, finish_send


def selection(rows_ref, count_ref, node_rows):
    rows = rows_ref[0, 0]
    parts, slots = rows.shape
    counts = jnp.broadcast_to(count_ref[0], (slots, parts)).T
    live = lax.broadcasted_iota(jnp.int32, (parts, slots), 1) < counts
    wanted = jnp.where(live, rows, -1)
    nodes = lax.broadcasted_iota(jnp.int32, (parts, slots, node_rows), 2)
    picked = wanted[:, :, None] == nodes
    return jnp.where(picked, 1.0, 0.0).astype(bf16).reshape(parts * slots, node_rows)


def tile_tables(from_ref, into_ref, live, from_blocks, cells):
    tiles = from_ref.shape[2]
    spare = cells

    def turned(row):
        return jnp.broadcast_to(row, (tiles, tiles)).T

    at = lax.broadcasted_iota(jnp.int32, (1, tiles), 1)
    key = jnp.where(at < live, into_ref[0] * from_blocks + from_ref[0], spare)
    key_down = turned(key)
    down = lax.broadcasted_iota(jnp.int32, (tiles, tiles), 0)
    across = lax.broadcasted_iota(jnp.int32, (tiles, tiles), 1)
    before = (key_down < key) | ((key_down == key) & (down < across))
    rank = jnp.sum(jnp.where(before, 1, 0), axis=0, keepdims=True)
    lands = turned(rank) == across
    order = jnp.sum(jnp.where(lands, down, 0), axis=0, keepdims=True)
    ordered_key = jnp.sum(jnp.where(lands, key_down, 0), axis=0, keepdims=True)
    cell = lax.broadcasted_iota(jnp.int32, (tiles, cells), 1)
    key_cells = jnp.broadcast_to(key, (cells, tiles)).T
    last = jnp.sum(jnp.where(key_cells <= cell, 1, 0), axis=0, keepdims=True) - 1
    found = jnp.sum(jnp.where(key_cells == cell, 1, 0), axis=0, keepdims=True)
    return order, ordered_key, last, found


def layer_kernel(feat_size, dom_size, tile, x_ref, ws_ref, wn_ref, rows_ref, count_ref, from_ref, into_ref,
                 live_ref, vals_ref, gain_ref, shift_ref, dh_ref,
                 hidden_ref, dself_ref, dneigh_ref, ggrad_ref, sgrad_ref,
                 xbuf, wnbuf, wsbuf, own, summed, neigh, halo, outgoing, pick, pick_t, ah, al, ah_t, al_t,
                 mg, back_out, returned, normed_buf, slope_buf, first, second, local_a, local_b,
                 scale_ref, vbuf, history, lists_v, lists_s,
                 local_sems, near_send, near_recv, sib_send, sib_recv,
                 send1, recv1, send2, recv2, send3, recv3, send4, recv4):
    me_f, me_d, me, total, peer_of = place(feat_size, dom_size)
    node_rows = x_ref.shape[2]
    columns, width = wn_ref.shape
    slots = rows_ref.shape[3]
    group_rows = dom_size * slots
    halo_rows = total * slots
    nodes = node_rows * total
    tiles = vbuf.shape[0]
    from_blocks = (node_rows + halo_rows) // tile
    into_blocks = node_rows // tile
    cells = into_blocks * from_blocks
    half = columns // 2
    side = lax.rem(me_d, 2)
    sibling = me_d + 1 - 2 * side
    mine_rows = pl.ds(pl.multiple_of(side * half, half), half)
    other_rows = pl.ds(pl.multiple_of((1 - side) * half, half), half)
    local_copies = [
        pltpu.make_async_copy(wn_ref, wnbuf.at[me_f], local_sems.at[0]),
        pltpu.make_async_copy(x_ref.at[me_f, 0], xbuf.at[me_f], local_sems.at[1]),
        pltpu.make_async_copy(ws_ref, wsbuf.at[me_f], local_sems.at[2]),
        pltpu.make_async_copy(vals_ref.at[0, 0], vbuf, local_sems.at[3]),
    ]
    for copy in local_copies:
        copy.start()

    def build_pick():
        pick[...] = selection(rows_ref, count_ref, node_rows)

        order, ordered_key, last, found = tile_tables(from_ref, into_ref, live_ref[0, 0], from_blocks, cells)
        lists_v[...] = jnp.zeros_like(lists_v)
        lists_v[0:1, 0:tiles] = order
        lists_v[1:2, 0:tiles] = ordered_key
        lists_v[2:3, 0:cells] = last
        lists_v[3:4, 0:cells] = found

    meet_all(total, peer_of, build_pick)

    def near(kind, k, arriving):
        other = lax.rem(me_f + k, feat_size)
        landing = other if arriving else me_f
        if kind == 1:
            source, target = x_ref.at[other, 0], xbuf.at[landing]
        else:
            source = (wn_ref, None, ws_ref)[kind].at[mine_rows]
            target = (wnbuf, None, wsbuf)[kind].at[landing, mine_rows]
        return pltpu.make_async_remote_copy(
            src_ref=source,
            dst_ref=target,
            send_sem=near_send.at[kind, other],
            recv_sem=near_recv.at[kind, landing],
            device_id=(other, me_d),
            device_id_type=MESH,
        )

    def passed(kind, k, arriving):
        other = lax.rem(me_f + k, feat_size)
        buffer = (wnbuf, None, wsbuf)[kind]
        return pltpu.make_async_remote_copy(
            src_ref=buffer.at[other, mine_rows],
            dst_ref=buffer.at[other, other_rows if arriving else mine_rows],
            send_sem=sib_send.at[kind, other],
            recv_sem=sib_recv.at[kind, other],
            device_id=(me_f, sibling),
            device_id_type=MESH,
        )

    for kind in range(3):
        for k in range(1, feat_size):
            near(kind, k, False).start()
    for k in range(1, feat_size):
        near(0, k, True).wait_recv()
        passed(0, k, False).start()
    for copy in local_copies:
        copy.wait()

    to_scalars = pltpu.make_async_copy(lists_v, lists_s, local_sems.at[4])
    to_scalars.start()
    to_scalars.wait()

    def add_tile(r, running):
        earlier = lists_s[1, jnp.maximum(r - 1, 0)]
        running = jnp.where(lists_s[1, r] == earlier, running, 0.0) + vbuf[lists_s[0, r]].astype(f32)
        history[r] = running
        return running

    lax.fori_loop(0, tiles, add_tile, jnp.zeros((tile, tile), f32), unroll=2)
    for b in range(into_blocks):
        span = slice(b * tile, (b + 1) * tile)

        def settle(s, weight):
            spot = b * from_blocks + s
            value = history[jnp.maximum(lists_s[2, spot], 0)]
            value = jnp.where(lists_s[3, spot] > 0, value, 0.0)
            high = value.astype(bf16)
            low = (value - high.astype(f32)).astype(bf16)
            lanes = pl.ds(pl.multiple_of(s * tile, tile), tile)
            ah[span, lanes] = high
            al[span, lanes] = low
            ah_t[lanes, span] = high.T
            al_t[lanes, span] = low.T
            return weight + value

        weight = lax.fori_loop(0, from_blocks, settle, jnp.zeros((tile, tile), f32))
        inverse_degree = 1.0 / (1.0 + jnp.sum(weight, axis=1, keepdims=True))
        scale_ref[span] = jnp.broadcast_to(inverse_degree, (tile, 128))
    summed[...] = jnp.dot(xbuf[me_f], wnbuf[me_f], preferred_element_type=f32)
    for k in range(1, feat_size):
        passed(0, k, True).wait_recv()
        near(1, k, True).wait_recv()
        other = lax.rem(me_f + k, feat_size)
        summed[...] += jnp.dot(xbuf[other], wnbuf[other], preferred_element_type=f32)
    neigh[...] = summed[...].astype(bf16)

    def slots_of(ref):
        return lambda peer: ref.at[pl.ds(pl.multiple_of(peer * slots, slots), slots)]

    mine = pl.ds(pl.multiple_of(me * slots, slots), slots)
    _, begin_group, finish_recv, finish_send1 = exchange(
        me, me_d, total, dom_size, peer_of, slots_of(outgoing), slots_of(halo), send1, recv1)
    for i in range(feat_size):
        group = lax.rem(me_f + i, feat_size)
        span = pl.ds(pl.multiple_of(group * group_rows, group_rows), group_rows)
        outgoing[span] = jnp.dot(pick[span], neigh[...], preferred_element_type=f32).astype(bf16)
        begin_group(group, 1 if i == 0 else 0)
    halo[mine] = outgoing[mine]
    for k in range(1, feat_size):
        near(2, k, True).wait_recv()
        passed(2, k, False).start()
    summed[...] = jnp.dot(ah[:, 0:node_rows], neigh[...], preferred_element_type=f32)
    summed[...] += jnp.dot(al[:, 0:node_rows], neigh[...], preferred_element_type=f32)
    own[...] = jnp.dot(xbuf[me_f], wsbuf[me_f], preferred_element_type=f32)
    for k in range(1, feat_size):
        passed(2, k, True).wait_recv()
        other = lax.rem(me_f + k, feat_size)
        own[...] += jnp.dot(xbuf[other], wsbuf[other], preferred_element_type=f32)

    def turn_pick(s, carry):
        rows = pl.ds(pl.multiple_of(s * tile, tile), tile)
        pick_t[:, rows] = pick[rows, :].T
        return carry

    lax.fori_loop(0, halo_rows // tile, turn_pick, 0)
    finish_recv()
    summed[...] += jnp.dot(ah[:, node_rows:], halo[...], preferred_element_type=f32)
    summed[...] += jnp.dot(al[:, node_rows:], halo[...], preferred_element_type=f32)
    blocks = node_rows // tile
    col_sum = jnp.zeros((1, width), f32)
    col_square = jnp.zeros((1, width), f32)
    for b in range(blocks):
        span = slice(b * tile, (b + 1) * tile)
        pre = own[span] + summed[span] * scale_ref[span, 0:1]
        own[span] = pre
        col_sum += jnp.sum(pre, axis=0, keepdims=True)
        col_square += jnp.sum(pre * pre, axis=0, keepdims=True)
    local_a[0:1] = col_sum
    local_a[1:2] = col_square
    first[me] = local_a[...]
    begin, _, finish_recv, finish_send2 = exchange(
        me, me_d, total, dom_size, peer_of, lambda peer: local_a, lambda peer: first.at[peer], send2, recv2)
    begin()
    finish_recv()
    sums = jnp.sum(first[...], axis=0)
    mean = sums[0:1] / nodes
    variance = sums[1:2] / nodes - mean * mean
    inverse = 1.0 / jnp.sqrt(variance + epsilon)
    gain = gain_ref[...].reshape(1, width)
    shift = shift_ref[...].reshape(1, width)
    slope_sum = jnp.zeros((1, width), f32)
    product_sum = jnp.zeros((1, width), f32)
    for b in range(blocks):
        span = slice(b * tile, (b + 1) * tile)
        normed = (own[span] - mean) * inverse
        act = gain * normed + shift
        logistic = jax.nn.sigmoid(act)
        hidden_ref[span] = (act * logistic).astype(bf16)
        slope = dh_ref[0, 0, span].astype(f32) * logistic * (1.0 + act * (1.0 - logistic))
        normed_buf[span] = normed
        slope_buf[span] = slope
        slope_sum += jnp.sum(slope, axis=0, keepdims=True)
        product_sum += jnp.sum(slope * normed, axis=0, keepdims=True)
    local_b[0:1] = slope_sum
    local_b[1:2] = product_sum
    second[me] = local_b[...]
    begin, _, finish_recv, finish_send3 = exchange(
        me, me_d, total, dom_size, peer_of, lambda peer: local_b, lambda peer: second.at[peer], send3, recv3)
    begin()
    finish_recv()
    sums = jnp.sum(second[...], axis=0)
    shift_grad = sums[0:1] / nodes
    gain_grad = sums[1:2] / nodes
    sgrad_ref[...] = shift_grad
    ggrad_ref[...] = gain_grad
    factor = gain * inverse
    for b in range(blocks):
        span = slice(b * tile, (b + 1) * tile)
        dpre = factor * (slope_buf[span] - shift_grad - normed_buf[span] * gain_grad)
        dself_ref[span] = dpre.astype(bf16)
        mg[span] = (dpre * scale_ref[span, 0:1]).astype(bf16)
    _, begin_group, finish_recv, finish_send4 = exchange(
        me, me_d, total, dom_size, peer_of, slots_of(back_out), slots_of(returned), send4, recv4)
    for i in range(feat_size):
        group = lax.rem(me_f + i, feat_size)
        span = pl.ds(pl.multiple_of(group * group_rows, group_rows), group_rows)
        edges = pl.ds(pl.multiple_of(node_rows + group * group_rows, tile), group_rows)
        back_out[span] = (
            jnp.dot(ah_t[edges], mg[...], preferred_element_type=f32)
            + jnp.dot(al_t[edges], mg[...], preferred_element_type=f32)
        ).astype(bf16)
        begin_group(group, 1 if i == 0 else 0)
    returned[mine] = back_out[mine]
    summed[...] = jnp.dot(ah_t[0:node_rows], mg[...], preferred_element_type=f32)
    summed[...] += jnp.dot(al_t[0:node_rows], mg[...], preferred_element_type=f32)
    for k in range(1, feat_size):
        for kind in range(3):
            near(kind, k, False).wait_send()
        passed(0, k, False).wait_send()
        passed(2, k, False).wait_send()
    finish_send1()
    finish_send2()
    finish_send3()
    finish_recv()
    added = jnp.dot(pick_t[...], returned[...], preferred_element_type=f32)
    dneigh_ref[...] = (summed[...] + added).astype(bf16)
    finish_send4()


def finish_kernel(*refs):
    count = len(refs) // 2
    for source, target in zip(refs[:count], refs[count:]):
        target[...] = source[...].reshape(target.shape)


def shards(feat_size, dom_size, features, w_self, w_neigh, gain, shift, d_hidden, send_rows, send_count,
           tile_src, tile_dst, tile_count, tile_vals):
    node_rows, columns = features.shape[2], features.shape[3]
    width = w_self.shape[1]
    tiles, tile = tile_vals.shape[2], tile_vals.shape[3]
    parts, slots = send_rows.shape[2], send_rows.shape[3]
    own_blocks = node_rows // tile
    halo_rows = parts * slots
    all_rows = node_rows + halo_rows
    cells = own_blocks * (all_rows // tile)
    list_lanes = -(-max(tiles, cells) // 128) * 128
    dma = pltpu.SemaphoreType.DMA
    shape = jax.ShapeDtypeStruct
    big = 60 * 1024 * 1024
    hidden, d_self, d_neigh, gain_grad, shift_grad = pl.pallas_call(
        functools.partial(layer_kernel, feat_size, dom_size, tile),
        out_shape=(
            shape((node_rows, width), bf16),
            shape((node_rows, width), bf16),
            shape((node_rows, width), bf16),
            shape((1, width), f32),
            shape((1, width), f32),
        ),
        in_specs=[ANY, ANY, ANY, VM, VM, VM, VM, SM, ANY, VM, VM, VM],
        out_specs=(VM,) * 5,
        scratch_shapes=[
            pltpu.VMEM((feat_size, node_rows, columns), bf16),
            pltpu.VMEM((feat_size, columns, width), bf16),
            pltpu.VMEM((feat_size, columns, width), bf16),
            pltpu.VMEM((node_rows, width), f32),
            pltpu.VMEM((node_rows, width), f32),
            pltpu.VMEM((node_rows, width), bf16),
            pltpu.VMEM((halo_rows, width), bf16),
            pltpu.VMEM((halo_rows, width), bf16),
            pltpu.VMEM((halo_rows, node_rows), bf16),
            pltpu.VMEM((node_rows, halo_rows), bf16),
            pltpu.VMEM((node_rows, all_rows), bf16),
            pltpu.VMEM((node_rows, all_rows), bf16),
            pltpu.VMEM((all_rows, node_rows), bf16),
            pltpu.VMEM((all_rows, node_rows), bf16),
            pltpu.VMEM((node_rows, width), bf16),
            pltpu.VMEM((halo_rows, width), bf16),
            pltpu.VMEM((halo_rows, width), bf16),
            pltpu.VMEM((node_rows, width), f32),
            pltpu.VMEM((node_rows, width), f32),
            pltpu.VMEM((parts, 2, width), f32),
            pltpu.VMEM((parts, 2, width), f32),
            pltpu.VMEM((2, width), f32),
            pltpu.VMEM((2, width), f32),
            pltpu.VMEM((node_rows, 128), f32),
            pltpu.VMEM((tiles, tile, tile), bf16),
            pltpu.VMEM((tiles, tile, tile), f32),
            pltpu.VMEM((8, list_lanes), jnp.int32),
            pltpu.SMEM((8, list_lanes), jnp.int32),
            dma((5,)), dma((3, feat_size)), dma((3, feat_size)), dma((3, feat_size)), dma((3, feat_size)),
        ] + [dma((parts,)) for _ in range(8)],
        compiler_params=pltpu.CompilerParams(collective_id=0, has_side_effects=True, vmem_limit_bytes=big),
        name="layer",
    )(features, w_self, w_neigh, send_rows, send_count, tile_src, tile_dst, tile_count, tile_vals, gain, shift, d_hidden)
    out_shape = (1, 1, node_rows, width)
    return pl.pallas_call(
        finish_kernel,
        out_shape=(shape(out_shape, bf16),) * 3 + (shape((width,), f32),) * 2,
        in_specs=[VM] * 5,
        out_specs=(VM,) * 5,
        name="finish",
    )(hidden, d_self, d_neigh, gain_grad, shift_grad)


def solution(mesh):
    in_specs = (
        P(None, "dom", None, "feat"),
        P("feat", None),
        P("feat", None),
        P(),
        P(),
        P("feat", "dom", None, None),
        P("feat", "dom", None, None),
        P("feat", "dom", None),
        P("feat", "dom", None),
        P("feat", "dom", None),
        P("feat", "dom"),
        P("feat", "dom", None, None, None),
    )
    out_specs = (
        P("feat", "dom", None, None),
        P("feat", "dom", None, None),
        P("feat", "dom", None, None),
        P(),
        P(),
    )
    body = functools.partial(shards, mesh.shape["feat"], mesh.shape["dom"])
    return jax.shard_map(body, mesh=mesh, in_specs=in_specs, out_specs=out_specs, check_vma=False)
```

```python
import functools

import jax
import jax.numpy as jnp
from jax import lax
from jax.experimental import pallas as pl
from jax.experimental.pallas import tpu as pltpu
from jax.sharding import PartitionSpec as P

epsilon = 1e-05
MESH = pl.DeviceIdType.MESH
VM = pl.BlockSpec(memory_space=pltpu.VMEM)
SM = pl.BlockSpec(memory_space=pltpu.SMEM)
ANY = pl.BlockSpec(memory_space=pl.ANY)
f32 = jnp.float32
bf16 = jnp.bfloat16


def place(feat_size, dom_size):
    me_f, me_d = lax.axis_index("feat"), lax.axis_index("dom")
    me = me_f * dom_size + me_d
    total = feat_size * dom_size

    def peer_of(k):
        peer = lax.rem(me + k, total)
        return peer, (lax.div(peer, dom_size), lax.rem(peer, dom_size))

    return me_f, me_d, me, total, peer_of


def meet_all(total, peer_of, while_waiting):
    barrier = pltpu.get_barrier_semaphore()

    def greet(k, carry):
        _, where = peer_of(k)
        pl.semaphore_signal(barrier, inc=1, device_id=where, device_id_type=MESH)
        return carry

    lax.fori_loop(1, total, greet, 0)
    while_waiting()
    pl.semaphore_wait(barrier, total - 1)


def exchange(me, me_d, total, dom_size, peer_of, source_of, target_of, send_sems, recv_sems):
    def copy(peer, where, landing):
        return pltpu.make_async_remote_copy(
            src_ref=source_of(peer),
            dst_ref=target_of(landing),
            send_sem=send_sems.at[peer],
            recv_sem=recv_sems.at[landing],
            device_id=where,
            device_id_type=MESH,
        )

    def begin_group(group, first):
        def start(k, carry):
            spot = lax.rem(me_d + k, dom_size)
            copy(group * dom_size + spot, (group, spot), me).start()
            return carry

        lax.fori_loop(first, dom_size, start, 0)

    def begin():
        def start(k, carry):
            peer, where = peer_of(k)
            copy(peer, where, me).start()
            return carry

        lax.fori_loop(1, total, start, 0)

    def finish_recv():
        def wait(k, carry):
            peer, where = peer_of(k)
            copy(peer, where, peer).wait_recv()
            return carry

        lax.fori_loop(1, total, wait, 0)

    def finish_group(group, first):
        def wait(k, carry):
            spot = lax.rem(me_d + k, dom_size)
            peer = group * dom_size + spot
            copy(peer, (group, spot), peer).wait_recv()
            return carry

        lax.fori_loop(first, dom_size, wait, 0)

    def finish_send():
        def wait(k, carry):
            peer, where = peer_of(k)
            copy(peer, where, me).wait_send()
            return carry

        lax.fori_loop(1, total, wait, 0)

    return begin, begin_group, finish_recv, finish_group, finish_send


def selection(rows_ref, count_ref, node_rows):
    rows = rows_ref[0, 0]
    parts, slots = rows.shape
    counts = jnp.broadcast_to(count_ref[0], (slots, parts)).T
    live = lax.broadcasted_iota(jnp.int32, (parts, slots), 1) < counts
    wanted = jnp.where(live, rows, -1)
    nodes = lax.broadcasted_iota(jnp.int32, (parts, slots, node_rows), 2)
    picked = wanted[:, :, None] == nodes
    return jnp.where(picked, 1.0, 0.0).astype(bf16).reshape(parts * slots, node_rows)


def tile_tables(from_ref, into_ref, live, from_blocks, cells):
    tiles = from_ref.shape[2]
    spare = cells

    def turned(row):
        return jnp.broadcast_to(row, (tiles, tiles)).T

    at = lax.broadcasted_iota(jnp.int32, (1, tiles), 1)
    key = jnp.where(at < live, into_ref[0] * from_blocks + from_ref[0], spare)
    key_down = turned(key)
    down = lax.broadcasted_iota(jnp.int32, (tiles, tiles), 0)
    across = lax.broadcasted_iota(jnp.int32, (tiles, tiles), 1)
    before = (key_down < key) | ((key_down == key) & (down < across))
    rank = jnp.sum(jnp.where(before, 1, 0), axis=0, keepdims=True)
    lands = turned(rank) == across
    order = jnp.sum(jnp.where(lands, down, 0), axis=0, keepdims=True)
    ordered_key = jnp.sum(jnp.where(lands, key_down, 0), axis=0, keepdims=True)
    cell = lax.broadcasted_iota(jnp.int32, (tiles, cells), 1)
    key_cells = jnp.broadcast_to(key, (cells, tiles)).T
    last = jnp.sum(jnp.where(key_cells <= cell, 1, 0), axis=0, keepdims=True) - 1
    found = jnp.sum(jnp.where(key_cells == cell, 1, 0), axis=0, keepdims=True)
    return order, ordered_key, last, found


def layer_kernel(feat_size, dom_size, tile, x_ref, ws_ref, wn_ref, rows_ref, count_ref, from_ref, into_ref,
                 live_ref, vals_ref, gain_ref, shift_ref, dh_ref,
                 hidden_ref, dself_ref, dneigh_ref, ggrad_ref, sgrad_ref,
                 xbuf, wnbuf, wsbuf, own, summed, neigh, halo, outgoing, pick, pick_t, ah, al, ah_t, al_t,
                 mg, back_out, returned, normed_buf, slope_buf, first, second, local_a, local_b,
                 scale_ref, vbuf, history, lists_v, lists_s,
                 local_sems, near_send, near_recv, sib_send, sib_recv,
                 send1, recv1, send2, recv2, send3, recv3, send4, recv4):
    me_f, me_d, me, total, peer_of = place(feat_size, dom_size)
    node_rows = x_ref.shape[2]
    columns, width = wn_ref.shape
    slots = rows_ref.shape[3]
    group_rows = dom_size * slots
    halo_rows = total * slots
    nodes = node_rows * total
    tiles = vbuf.shape[0]
    from_blocks = (node_rows + halo_rows) // tile
    into_blocks = node_rows // tile
    cells = into_blocks * from_blocks
    half = columns // 2
    side = lax.rem(me_d, 2)
    sibling = me_d + 1 - 2 * side
    mine_rows = pl.ds(pl.multiple_of(side * half, half), half)
    other_rows = pl.ds(pl.multiple_of((1 - side) * half, half), half)
    local_copies = [
        pltpu.make_async_copy(wn_ref, wnbuf.at[me_f], local_sems.at[0]),
        pltpu.make_async_copy(x_ref.at[me_f, 0], xbuf.at[me_f], local_sems.at[1]),
        pltpu.make_async_copy(ws_ref, wsbuf.at[me_f], local_sems.at[2]),
        pltpu.make_async_copy(vals_ref.at[0, 0], vbuf, local_sems.at[3]),
    ]
    for copy in local_copies:
        copy.start()

    def build_pick():
        pick[...] = selection(rows_ref, count_ref, node_rows)

        order, ordered_key, last, found = tile_tables(from_ref, into_ref, live_ref[0, 0], from_blocks, cells)
        lists_v[...] = jnp.zeros_like(lists_v)
        lists_v[0:1, 0:tiles] = order
        lists_v[1:2, 0:tiles] = ordered_key
        lists_v[2:3, 0:cells] = last
        lists_v[3:4, 0:cells] = found

    meet_all(total, peer_of, build_pick)

    def near(kind, k, arriving):
        other = lax.rem(me_f + k, feat_size)
        landing = other if arriving else me_f
        if kind == 1:
            source, target = x_ref.at[other, 0], xbuf.at[landing]
        else:
            source = (wn_ref, None, ws_ref)[kind].at[mine_rows]
            target = (wnbuf, None, wsbuf)[kind].at[landing, mine_rows]
        return pltpu.make_async_remote_copy(
            src_ref=source,
            dst_ref=target,
            send_sem=near_send.at[kind, other],
            recv_sem=near_recv.at[kind, landing],
            device_id=(other, me_d),
            device_id_type=MESH,
        )

    def passed(kind, k, arriving):
        other = lax.rem(me_f + k, feat_size)
        buffer = (wnbuf, None, wsbuf)[kind]
        return pltpu.make_async_remote_copy(
            src_ref=buffer.at[other, mine_rows],
            dst_ref=buffer.at[other, other_rows if arriving else mine_rows],
            send_sem=sib_send.at[kind, other],
            recv_sem=sib_recv.at[kind, other],
            device_id=(me_f, sibling),
            device_id_type=MESH,
        )

    for kind in range(3):
        for k in range(1, feat_size):
            near(kind, k, False).start()
    for k in range(1, feat_size):
        near(0, k, True).wait_recv()
        passed(0, k, False).start()
    for copy in local_copies:
        copy.wait()

    to_scalars = pltpu.make_async_copy(lists_v, lists_s, local_sems.at[4])
    to_scalars.start()
    to_scalars.wait()

    def add_tile(r, running):
        earlier = lists_s[1, jnp.maximum(r - 1, 0)]
        running = jnp.where(lists_s[1, r] == earlier, running, 0.0) + vbuf[lists_s[0, r]].astype(f32)
        history[r] = running
        return running

    lax.fori_loop(0, tiles, add_tile, jnp.zeros((tile, tile), f32), unroll=2)
    for b in range(into_blocks):
        span = slice(b * tile, (b + 1) * tile)

        def settle(s, weight):
            spot = b * from_blocks + s
            value = history[jnp.maximum(lists_s[2, spot], 0)]
            value = jnp.where(lists_s[3, spot] > 0, value, 0.0)
            high = value.astype(bf16)
            low = (value - high.astype(f32)).astype(bf16)
            lanes = pl.ds(pl.multiple_of(s * tile, tile), tile)
            ah[span, lanes] = high
            al[span, lanes] = low
            ah_t[lanes, span] = high.T
            al_t[lanes, span] = low.T
            return weight + value

        weight = lax.fori_loop(0, from_blocks, settle, jnp.zeros((tile, tile), f32))
        inverse_degree = 1.0 / (1.0 + jnp.sum(weight, axis=1, keepdims=True))
        scale_ref[span] = jnp.broadcast_to(inverse_degree, (tile, 128))
    summed[...] = jnp.dot(xbuf[me_f], wnbuf[me_f], preferred_element_type=f32)
    for k in range(1, feat_size):
        passed(0, k, True).wait_recv()
        near(1, k, True).wait_recv()
        other = lax.rem(me_f + k, feat_size)
        summed[...] += jnp.dot(xbuf[other], wnbuf[other], preferred_element_type=f32)
    neigh[...] = summed[...].astype(bf16)

    def slots_of(ref):
        return lambda peer: ref.at[pl.ds(pl.multiple_of(peer * slots, slots), slots)]

    mine = pl.ds(pl.multiple_of(me * slots, slots), slots)
    _, begin_group, _, finish_group, finish_send1 = exchange(
        me, me_d, total, dom_size, peer_of, slots_of(outgoing), slots_of(halo), send1, recv1)
    for i in range(feat_size):
        group = lax.rem(me_f + i, feat_size)
        span = pl.ds(pl.multiple_of(group * group_rows, group_rows), group_rows)
        outgoing[span] = jnp.dot(pick[span], neigh[...], preferred_element_type=f32).astype(bf16)
        begin_group(group, 1 if i == 0 else 0)
    halo[mine] = outgoing[mine]
    for k in range(1, feat_size):
        near(2, k, True).wait_recv()
        passed(2, k, False).start()
    summed[...] = jnp.dot(ah[:, 0:node_rows], neigh[...], preferred_element_type=f32)
    summed[...] += jnp.dot(al[:, 0:node_rows], neigh[...], preferred_element_type=f32)
    own[...] = jnp.dot(xbuf[me_f], wsbuf[me_f], preferred_element_type=f32)
    for k in range(1, feat_size):
        passed(2, k, True).wait_recv()
        other = lax.rem(me_f + k, feat_size)
        own[...] += jnp.dot(xbuf[other], wsbuf[other], preferred_element_type=f32)

    def turn_pick(s, carry):
        rows = pl.ds(pl.multiple_of(s * tile, tile), tile)
        pick_t[:, rows] = pick[rows, :].T
        return carry

    lax.fori_loop(0, halo_rows // tile, turn_pick, 0)
    for i in range(feat_size):
        group = lax.rem(me_f + feat_size - i, feat_size)
        span = pl.ds(pl.multiple_of(group * group_rows, group_rows), group_rows)
        edges = pl.ds(pl.multiple_of(node_rows + group * group_rows, tile), group_rows)
        finish_group(group, 1 if i == 0 else 0)
        summed[...] += (
            jnp.dot(ah[:, edges], halo[span], preferred_element_type=f32)
            + jnp.dot(al[:, edges], halo[span], preferred_element_type=f32)
        )
    blocks = node_rows // tile
    col_sum = jnp.zeros((1, width), f32)
    col_square = jnp.zeros((1, width), f32)
    for b in range(blocks):
        span = slice(b * tile, (b + 1) * tile)
        pre = own[span] + summed[span] * scale_ref[span, 0:1]
        own[span] = pre
        col_sum += jnp.sum(pre, axis=0, keepdims=True)
        col_square += jnp.sum(pre * pre, axis=0, keepdims=True)
    local_a[0:1] = col_sum
    local_a[1:2] = col_square
    first[me] = local_a[...]
    begin, _, finish_recv, _, finish_send2 = exchange(
        me, me_d, total, dom_size, peer_of, lambda peer: local_a, lambda peer: first.at[peer], send2, recv2)
    begin()
    finish_recv()
    sums = jnp.sum(first[...], axis=0)
    mean = sums[0:1] / nodes
    variance = sums[1:2] / nodes - mean * mean
    inverse = 1.0 / jnp.sqrt(variance + epsilon)
    gain = gain_ref[...].reshape(1, width)
    shift = shift_ref[...].reshape(1, width)
    slope_sum = jnp.zeros((1, width), f32)
    product_sum = jnp.zeros((1, width), f32)
    for b in range(blocks):
        span = slice(b * tile, (b + 1) * tile)
        normed = (own[span] - mean) * inverse
        act = gain * normed + shift
        logistic = jax.nn.sigmoid(act)
        hidden_ref[span] = (act * logistic).astype(bf16)
        slope = dh_ref[0, 0, span].astype(f32) * logistic * (1.0 + act * (1.0 - logistic))
        normed_buf[span] = normed
        slope_buf[span] = slope
        slope_sum += jnp.sum(slope, axis=0, keepdims=True)
        product_sum += jnp.sum(slope * normed, axis=0, keepdims=True)
    local_b[0:1] = slope_sum
    local_b[1:2] = product_sum
    second[me] = local_b[...]
    begin, _, finish_recv, _, finish_send3 = exchange(
        me, me_d, total, dom_size, peer_of, lambda peer: local_b, lambda peer: second.at[peer], send3, recv3)
    begin()
    finish_recv()
    sums = jnp.sum(second[...], axis=0)
    shift_grad = sums[0:1] / nodes
    gain_grad = sums[1:2] / nodes
    sgrad_ref[...] = shift_grad
    ggrad_ref[...] = gain_grad
    factor = gain * inverse
    for b in range(blocks):
        span = slice(b * tile, (b + 1) * tile)
        dpre = factor * (slope_buf[span] - shift_grad - normed_buf[span] * gain_grad)
        dself_ref[span] = dpre.astype(bf16)
        mg[span] = (dpre * scale_ref[span, 0:1]).astype(bf16)
    _, begin_group, _, finish_group, finish_send4 = exchange(
        me, me_d, total, dom_size, peer_of, slots_of(back_out), slots_of(returned), send4, recv4)
    for i in range(feat_size):
        group = lax.rem(me_f + i, feat_size)
        span = pl.ds(pl.multiple_of(group * group_rows, group_rows), group_rows)
        edges = pl.ds(pl.multiple_of(node_rows + group * group_rows, tile), group_rows)
        back_out[span] = (
            jnp.dot(ah_t[edges], mg[...], preferred_element_type=f32)
            + jnp.dot(al_t[edges], mg[...], preferred_element_type=f32)
        ).astype(bf16)
        begin_group(group, 1 if i == 0 else 0)
    returned[mine] = back_out[mine]
    summed[...] = jnp.dot(ah_t[0:node_rows], mg[...], preferred_element_type=f32)
    summed[...] += jnp.dot(al_t[0:node_rows], mg[...], preferred_element_type=f32)
    for k in range(1, feat_size):
        for kind in range(3):
            near(kind, k, False).wait_send()
        passed(0, k, False).wait_send()
        passed(2, k, False).wait_send()
    finish_send1()
    finish_send2()
    finish_send3()
    for i in range(feat_size):
        group = lax.rem(me_f + feat_size - i, feat_size)
        span = pl.ds(pl.multiple_of(group * group_rows, group_rows), group_rows)
        finish_group(group, 1 if i == 0 else 0)
        gathered = jnp.dot(pick_t[:, span], returned[span], preferred_element_type=f32)
        if i < feat_size - 1:
            summed[...] += gathered
        else:
            dneigh_ref[...] = (summed[...] + gathered).astype(bf16)
    finish_send4()


def finish_kernel(*refs):
    count = len(refs) // 2
    for source, target in zip(refs[:count], refs[count:]):
        target[...] = source[...].reshape(target.shape)


def shards(feat_size, dom_size, features, w_self, w_neigh, gain, shift, d_hidden, send_rows, send_count,
           tile_src, tile_dst, tile_count, tile_vals):
    node_rows, columns = features.shape[2], features.shape[3]
    width = w_self.shape[1]
    tiles, tile = tile_vals.shape[2], tile_vals.shape[3]
    parts, slots = send_rows.shape[2], send_rows.shape[3]
    own_blocks = node_rows // tile
    halo_rows = parts * slots
    all_rows = node_rows + halo_rows
    cells = own_blocks * (all_rows // tile)
    list_lanes = -(-max(tiles, cells) // 128) * 128
    dma = pltpu.SemaphoreType.DMA
    shape = jax.ShapeDtypeStruct
    big = 60 * 1024 * 1024
    hidden, d_self, d_neigh, gain_grad, shift_grad = pl.pallas_call(
        functools.partial(layer_kernel, feat_size, dom_size, tile),
        out_shape=(
            shape((node_rows, width), bf16),
            shape((node_rows, width), bf16),
            shape((node_rows, width), bf16),
            shape((1, width), f32),
            shape((1, width), f32),
        ),
        in_specs=[ANY, ANY, ANY, VM, VM, VM, VM, SM, ANY, VM, VM, VM],
        out_specs=(VM,) * 5,
        scratch_shapes=[
            pltpu.VMEM((feat_size, node_rows, columns), bf16),
            pltpu.VMEM((feat_size, columns, width), bf16),
            pltpu.VMEM((feat_size, columns, width), bf16),
            pltpu.VMEM((node_rows, width), f32),
            pltpu.VMEM((node_rows, width), f32),
            pltpu.VMEM((node_rows, width), bf16),
            pltpu.VMEM((halo_rows, width), bf16),
            pltpu.VMEM((halo_rows, width), bf16),
            pltpu.VMEM((halo_rows, node_rows), bf16),
            pltpu.VMEM((node_rows, halo_rows), bf16),
            pltpu.VMEM((node_rows, all_rows), bf16),
            pltpu.VMEM((node_rows, all_rows), bf16),
            pltpu.VMEM((all_rows, node_rows), bf16),
            pltpu.VMEM((all_rows, node_rows), bf16),
            pltpu.VMEM((node_rows, width), bf16),
            pltpu.VMEM((halo_rows, width), bf16),
            pltpu.VMEM((halo_rows, width), bf16),
            pltpu.VMEM((node_rows, width), f32),
            pltpu.VMEM((node_rows, width), f32),
            pltpu.VMEM((parts, 2, width), f32),
            pltpu.VMEM((parts, 2, width), f32),
            pltpu.VMEM((2, width), f32),
            pltpu.VMEM((2, width), f32),
            pltpu.VMEM((node_rows, 128), f32),
            pltpu.VMEM((tiles, tile, tile), bf16),
            pltpu.VMEM((tiles, tile, tile), f32),
            pltpu.VMEM((8, list_lanes), jnp.int32),
            pltpu.SMEM((8, list_lanes), jnp.int32),
            dma((5,)), dma((3, feat_size)), dma((3, feat_size)), dma((3, feat_size)), dma((3, feat_size)),
        ] + [dma((parts,)) for _ in range(8)],
        compiler_params=pltpu.CompilerParams(collective_id=0, has_side_effects=True, vmem_limit_bytes=big),
        name="layer",
    )(features, w_self, w_neigh, send_rows, send_count, tile_src, tile_dst, tile_count, tile_vals, gain, shift, d_hidden)
    out_shape = (1, 1, node_rows, width)
    return pl.pallas_call(
        finish_kernel,
        out_shape=(shape(out_shape, bf16),) * 3 + (shape((width,), f32),) * 2,
        in_specs=[VM] * 5,
        out_specs=(VM,) * 5,
        name="finish",
    )(hidden, d_self, d_neigh, gain_grad, shift_grad)


def solution(mesh):
    in_specs = (
        P(None, "dom", None, "feat"),
        P("feat", None),
        P("feat", None),
        P(),
        P(),
        P("feat", "dom", None, None),
        P("feat", "dom", None, None),
        P("feat", "dom", None),
        P("feat", "dom", None),
        P("feat", "dom", None),
        P("feat", "dom"),
        P("feat", "dom", None, None, None),
    )
    out_specs = (
        P("feat", "dom", None, None),
        P("feat", "dom", None, None),
        P("feat", "dom", None, None),
        P(),
        P(),
    )
    body = functools.partial(shards, mesh.shape["feat"], mesh.shape["dom"])
    return jax.shard_map(body, mesh=mesh, in_specs=in_specs, out_specs=out_specs, check_vma=False)
```
